256 devices in a mesh: leaf: 4 (over x), row: 64 (over y, z, core).
Axes of the slice: x: 4, y: 4, z: 8, core: 2. Of those that a mesh axis runs over, the one named last changes fastest.
Arguments:
- right_side: bfloat16 [4, 256, 256, 512], P('leaf', 'row'), may hold values from -6 to 6
- panels: bfloat16 [4, 4, 256, 512, 512], P(None, 'leaf', 'row'), may hold values from -0.1875 to 0.1875
- tile_counts: int32 [4, 4, 256], P(None, 'leaf', 'row'), may hold values from 0 to 512, as said below
- diag_leaf: bfloat16 [4, 512, 512], P('leaf')
- diag_pair: bfloat16 [2, 512, 512], replicated
- diag_root: bfloat16 [2, 512, 512], replicated
- sup_rows: int32 [4], replicated, may hold values from 0 to 255, as said below
Outputs:
- solution: bfloat16 [4, 4, 256, 512], P(None, 'leaf')
- updated_side: bfloat16 [256, 256, 512], P('row')
The draws below stay inside these ranges and needn't reach their ends.
Inputs may be any that keep to these rules, and one draw needn't show every extreme that they name: `sup_rows`: 4 distinct block rows, one a level. `tile_counts`: 0 marks a tile with no valid columns.
All inputs are finite; a program needn't handle non-finite values.
Results may differ from the reference program's by a relative error of at most 0.0062.
Values may be sent and summed in bfloat16 or wider, within the bound.
A program may use at most 128 MiB of HBM per device.

```python
import jax
import jax.numpy as jnp
from jax import lax

W = 512
R = 256
LEVELS = 4
TILES = 256
N_LEAF = 4


def near_identity(key, count):
    first_key = jax.random.fold_in(key, 0)
    noise = jax.random.normal(first_key, (count, W, W), jnp.float32) * (0.5 / W ** 0.5)
    return (jnp.eye(W, dtype=jnp.float32)[None] + noise).astype(jnp.bfloat16)


def draw_diag_leaf(key, part):
    return near_identity(jax.random.fold_in(key, 11), N_LEAF)


def draw_diag_pair(key, part):
    return near_identity(jax.random.fold_in(key, 12), N_LEAF // 2)


def draw_diag_root(key, part):
    return near_identity(jax.random.fold_in(key, 13), 2)


def draw_sup_rows(key, part):
    first_key, second_key = jax.random.split(jax.random.fold_in(key, 21))
    middle = jax.random.permutation(first_key, TILES - 2)[:LEVELS - 2] + 1
    picked_tiles = jnp.concatenate([jnp.array([0, TILES - 1], jnp.int32), middle.astype(jnp.int32)])
    shuffle = jax.random.permutation(second_key, LEVELS)
    return picked_tiles[shuffle].astype(jnp.int32)


def draw_tile_counts(key, part):
    first_key, second_key, third_key = jax.random.split(jax.random.fold_in(key, 31), 3)
    shape_all = (LEVELS, N_LEAF, TILES)
    counts_all = jax.random.randint(first_key, shape_all, 1, W + 1)
    empty_tile = jax.random.randint(second_key, shape_all, 0, 4) == 0
    counts_all = jnp.where(empty_tile, 0, counts_all).reshape(-1)
    chosen_slots = jax.random.permutation(third_key, LEVELS * N_LEAF * TILES)[:2]
    counts_all = counts_all.at[chosen_slots[0]].set(0).at[chosen_slots[1]].set(W)
    return counts_all.reshape(shape_all).astype(jnp.int32)


def level_of(own_key, shape, cuts, least, top_value):
    gain, own = 1.0, jax.random.fold_in(own_key, 6)
    for position, parts in cuts:
        steps = jnp.exp(jax.random.uniform(jax.random.fold_in(own, position), (parts,), jnp.float32, least / len(cuts), top_value / len(cuts)))
        gain = gain * jnp.repeat(steps, shape[position] // parts).reshape([-1 if axis == position else 1 for axis in range(len(shape))])
    return gain


def bell_draw(own_key, dims, width, most, cuts=(), held_as=jnp.bfloat16):
    result = width * jax.random.normal(own_key, dims, jnp.float32)
    if cuts:
        result = result * level_of(own_key, dims, cuts, -0.22, 0.18)
    return jnp.clip(result, -most, most).astype(held_as)


def setup_inputs(seed: int = 0) -> dict:
    key_of = jax.random.split(jax.random.key(seed), 8)
    right_side = bell_draw(key_of[0], (N_LEAF, TILES, R, W), 1.0, 6.0, ((0, 4), (1, 64)))
    panels = bell_draw(key_of[1], (LEVELS, N_LEAF, TILES, W, W), (2 * W) ** -0.5, 0.1875, ((1, 4), (2, 64)))
    tile_counts = draw_tile_counts(jax.random.fold_in(key_of[7], 71), 0)
    diag_leaf = draw_diag_leaf(jax.random.fold_in(key_of[7], 71), 0)
    diag_pair = draw_diag_pair(jax.random.fold_in(key_of[7], 71), 0)
    diag_root = draw_diag_root(jax.random.fold_in(key_of[7], 71), 0)
    sup_rows = draw_sup_rows(jax.random.fold_in(key_of[7], 71), 0)
    return dict(right_side=right_side, panels=panels, tile_counts=tile_counts, diag_leaf=diag_leaf, diag_pair=diag_pair, diag_root=diag_root, sup_rows=sup_rows)


def reference(right_side, panels, tile_counts, diag_leaf, diag_pair, diag_root, sup_rows):
    share_parts = right_side.astype(jnp.float32)
    totals = jnp.zeros(share_parts.shape, jnp.float32)
    tile_ids = jnp.arange(TILES, dtype=jnp.int32)
    columns = jnp.arange(W, dtype=jnp.int32)
    solved = []
    for panel_height in range(LEVELS):
        target_row = sup_rows[panel_height]
        partial_result = lax.dynamic_index_in_dim(share_parts, target_row, 1, keepdims=False) - lax.dynamic_index_in_dim(totals, target_row, 1, keepdims=False)
        if panel_height == 0:
            merged = partial_result
            inverse = diag_leaf
        elif panel_height == 1:
            merged = partial_result + partial_result[jnp.array([1, 0, 3, 2])]
            inverse = diag_pair[jnp.array([0, 0, 1, 1])]
        else:
            merged = jnp.broadcast_to(jnp.sum(partial_result, axis=0), partial_result.shape)
            inverse = jnp.broadcast_to(diag_root[panel_height - 2], (N_LEAF, W, W))
        rounded = lax.optimization_barrier(merged.astype(jnp.bfloat16)).astype(jnp.float32)
        current_solved = jnp.einsum("srw,swv->srv", rounded, inverse.astype(jnp.float32)).astype(jnp.bfloat16)
        solved.append(current_solved)
        structure = jnp.logical_not(jnp.any(tile_ids[:, None] == sup_rows[: panel_height + 1][None, :], axis=1))
        for current_leaf in range(N_LEAF):
            update_term = jnp.einsum("pi,bis->bps", current_solved[current_leaf].astype(jnp.float32), panels[panel_height, current_leaf].astype(jnp.float32))
            col_mask = (columns[None, :] < tile_counts[panel_height, current_leaf][:, None]) & structure[:, None]
            totals = totals.at[current_leaf].add(update_term * col_mask[:, None, :].astype(jnp.float32))
    solution = jnp.stack(solved)
    updated_side = jnp.sum(share_parts - totals, axis=0).astype(jnp.bfloat16)
    return solution, updated_side
```

```python
import functools

import jax
import jax.numpy as jnp
from jax import lax
from jax.experimental import pallas as pl
from jax.experimental.pallas import tpu as pltpu
from jax.sharding import PartitionSpec as P

MESH = pl.DeviceIdType.MESH
F32, BF16 = jnp.float32, jnp.bfloat16
ROUNDS = ((0,), (1,), (2,), (3,))
GRIDS = {64: (4, 8, 2), 8: (2, 2, 2)}
SEMS = 96


def kernel(grid, n_leaf, sup, cnt, rs_h, pan_h, dl_h, dp_h, dr_h, sol_o, upd_o, *scratch):
    ny, nz, nc = grid
    (rs, pan, dl, dp, dr, held, qacc, sol, base, xr, fin, rest, sem) = scratch
    levels, (tiles, wide, _) = len(pan), pan[0].shape
    rhs = rs.shape[1]
    low = wide // ny
    x, r = lax.axis_index("leaf"), lax.axis_index("row")
    y, z, c = r // (nz * nc), (r // nc) % nz, r % nc
    used = [0]
    drains = []

    def device(x_, y_, z_, c_):
        return (x_, (y_ * nz + z_) * nc + c_)

    def fresh():
        used[0] += 1
        assert used[0] <= SEMS
        return sem.at[used[0] - 1]

    def fetch(src, dst):
        copy = pltpu.make_async_copy(src, dst, fresh())
        copy.start()
        return copy

    def exchange(copies, whole):
        out, got = fresh(), fresh()
        for src, dst, dev in copies:
            pltpu.make_async_remote_copy(
                src_ref=src, dst_ref=dst, send_sem=out, recv_sem=got, device_id=dev, device_id_type=MESH
            ).start()
        drains.append(pltpu.make_async_copy(whole, whole, out))
        return pltpu.make_async_copy(whole, whole, got)

    ready = {"rs": fetch(rs_h.at[0], rs), "d0": fetch(dl_h, dl)}
    ready["p0"] = fetch(pan_h.at[0, 0], pan[0])
    ready["d1"] = fetch(dp_h, dp)
    ready["p1"] = fetch(pan_h.at[1, 0], pan[1])
    ready["d2"] = fetch(dr_h, dr)
    ready["p2"] = fetch(pan_h.at[2, 0], pan[2])
    ready["p3"] = fetch(pan_h.at[3, 0], pan[3])
    waited = set()

    def need(name):
        if name not in waited:
            waited.add(name)
            ready[name].wait()

    barrier = pltpu.get_barrier_semaphore()
    peers = [device(x, y, z, 1 - c)]
    peers += [device(x, y, (z + k) % nz, c) for k in range(1, nz)]
    peers += [device(x ^ i, (y + j) % ny, z, c) for i in range(n_leaf) for j in range(ny) if i or j]
    for dev in peers:
        pl.semaphore_signal(barrier, inc=1, device_id=dev, device_id_type=MESH)
    pl.semaphore_wait(barrier, len(peers))

    owner = [jnp.where(lax.div(sup[m], tiles) == r, 1.0, 0.0).astype(F32) for m in range(levels)]
    local = [lax.rem(sup[m], tiles) for m in range(levels)]
    columns = lax.broadcasted_iota(jnp.int32, (1, wide), 1)

    def product(level, tile, count):
        done = sol[level].reshape(rhs, wide)
        term = jnp.dot(done, pan[level][tile], preferred_element_type=F32)
        return jnp.where(columns < count, term, 0.0)

    def bulk(level):
        def one(tile, carry):
            count = cnt[level, 0, tile]
            for m in range(level + 1):
                count = jnp.where(sup[m] == r * tiles + tile, 0, count)
            term = product(level, tile, count)
            before = rs[tile].astype(F32) if level == 0 else held[tile]
            held[tile] = before - term
            return carry

        lax.fori_loop(0, tiles, one, 0)

    inverses = [("d0", lambda: dl[0]), ("d1", lambda: dp[x // 2]), ("d2", lambda: dr[0]), ("d2", lambda: dr[1])]
    late = []
    for number, group in enumerate(ROUNDS):
        qs, qr, zs, zr, ys, yr = rest[number][:6]
        size = len(group)
        need("rs")
        for i, m in enumerate(group):
            part = rs[local[m]].astype(F32)
            if number:
                part = part - qacc[m]
            part = (part * owner[m]).astype(BF16)
            for half in range(nc):
                qs[half, i] = part[half * (rhs // nc) : (half + 1) * (rhs // nc)]
        exchange([(qs.at[1 - c], qr, device(x, y, z, 1 - c))], qr).wait()
        for i in range(size):
            both = qs[c, i].astype(F32) + qr[i].astype(F32)
            zs[:, i] = both.astype(BF16).reshape(nz, rhs // nc // nz, wide)
        arrival = exchange(
            [(zs.at[(z + k) % nz], zr.at[k - 1], device(x, y, (z + k) % nz, c)) for k in range(1, nz)], zr
        )
        for level in late:
            bulk(level)
        late = []
        arrival.wait()
        rows = zs[z].astype(F32)
        for k in range(nz - 1):
            rows = rows + zr[k].astype(F32)
        rows = rows.astype(BF16)
        for k in range(ny):
            ys[k] = rows[:, :, k * low : (k + 1) * low]
        exchange(
            [(ys.at[(y + k) % ny], yr.at[k - 1], device(x, (y + k) % ny, z, c)) for k in range(1, ny)], yr
        ).wait()
        piece = ys[y].astype(F32)
        for k in range(ny - 1):
            piece = piece + yr[k].astype(F32)
        spreads = []
        for i, m in enumerate(group):
            n = (1, 2, n_leaf, n_leaf)[m]
            cs, cr = rest[number][6 + i]
            own = (x % n) * ny + y
            cs[...] = piece[i]
            cr[own] = piece[i]
            exchange(
                [
                    (cs, cr.at[own], device(x ^ a, (y + b) % ny, z, c))
                    for a in range(n)
                    for b in range(ny)
                    if a or b
                ],
                cr.at[pl.ds(0, n * ny - 1)],
            ).wait()
            merged = []
            for k in range(ny):
                total = cr[k]
                for a in range(1, n):
                    total = total + cr[a * ny + k]
                merged.append(total.astype(BF16))
            merged = jnp.concatenate(merged, axis=1)
            name, inverse = inverses[m]
            need(name)
            sol[m, c, z] = jnp.dot(merged, inverse(), preferred_element_type=F32).astype(BF16)
            spreads.append(
                exchange(
                    [
                        (sol.at[m, c, z], sol.at[m, c, z], device(x, y, (z + k) % nz, c))
                        for k in range(1, nz)
                    ],
                    sol.at[m, c, pl.ds(0, nz - 1)],
                )
            )
        for m, spread in zip(group, spreads):
            spread.wait()
            exchange([(sol.at[m, c], sol.at[m, c], device(x, y, z, 1 - c))], sol.at[m, c]).wait()
            drains.append(fetch(sol.at[m], sol_o.at[m]))
        for m in group:
            need(f"p{m}")
            later = [k for rest_group in ROUNDS[number + 1 :] for k in rest_group]
            for k in later:
                term = product(m, local[k], cnt[m, 0, local[k]])
                qacc[k] = term if m == 0 else qacc[k] + term
        late = list(group)

    for level in late:
        bulk(level)
    for tile in range(tiles):
        base[tile] = held[tile].astype(BF16)
    exchange([(base.at[x ^ k], xr.at[k - 1], device(x ^ k, y, z, c)) for k in range(1, n_leaf)], xr).wait()
    total = held[x]
    for k in range(n_leaf - 1):
        total = total + xr[k].astype(F32)
    fin[...] = total.astype(BF16)
    arrival = exchange(
        [(fin, upd_o.at[x], device(x ^ k, y, z, c)) for k in range(1, n_leaf)], upd_o.at[pl.ds(0, n_leaf - 1)]
    )
    drains.append(fetch(fin, upd_o.at[x]))
    arrival.wait()
    for copy in drains:
        copy.wait()


def on_device(grid, n_leaf, right_side, panels, tile_counts, diag_leaf, diag_pair, diag_root, sup_rows):
    ny, nz, nc = grid
    levels, _, tiles, wide, _ = panels.shape
    rhs = right_side.shape[2]
    part, low = rhs // nc // nz, wide // ny
    rest = []
    for group in ROUNDS:
        size = len(group)
        bufs = [
            pltpu.VMEM((nc, size, rhs // nc, wide), BF16),
            pltpu.VMEM((size, rhs // nc, wide), BF16),
            pltpu.VMEM((nz, size, part, wide), BF16),
            pltpu.VMEM((nz - 1, size, part, wide), BF16),
            pltpu.VMEM((ny, size, part, low), BF16),
            pltpu.VMEM((ny - 1, size, part, low), BF16),
        ]
        for m in group:
            n = (1, 2, n_leaf, n_leaf)[m]
            bufs.append([pltpu.VMEM((part, low), F32), pltpu.VMEM((n * ny, part, low), F32)])
        rest.append(bufs)
    scratch = [
        pltpu.VMEM((tiles, rhs, wide), BF16),
        [pltpu.VMEM((tiles, wide, wide), BF16)] * levels,
        pltpu.VMEM((1, wide, wide), BF16),
        pltpu.VMEM((2, wide, wide), BF16),
        pltpu.VMEM((2, wide, wide), BF16),
        pltpu.VMEM((tiles, rhs, wide), F32),
        pltpu.VMEM((levels, rhs, wide), F32),
        pltpu.VMEM((levels, nc, nz, part, wide), BF16),
        pltpu.VMEM((tiles, rhs, wide), BF16),
        pltpu.VMEM((n_leaf - 1, rhs, wide), BF16),
        pltpu.VMEM((rhs, wide), BF16),
        rest,
        pltpu.SemaphoreType.DMA((SEMS,)),
    ]
    anywhere, scalars = pl.BlockSpec(memory_space=pl.ANY), pl.BlockSpec(memory_space=pltpu.SMEM)
    solved, updated = pl.pallas_call(
        functools.partial(kernel, grid, n_leaf),
        out_shape=(
            jax.ShapeDtypeStruct((levels, nc, nz, part, wide), BF16),
            jax.ShapeDtypeStruct((tiles, rhs, wide), BF16),
        ),
        in_specs=[scalars, scalars] + [anywhere] * 5,
        out_specs=(anywhere, anywhere),
        scratch_shapes=scratch,
        compiler_params=pltpu.CompilerParams(
            collective_id=0, has_side_effects=True, vmem_limit_bytes=56 * 2**20
        ),
    )(sup_rows, tile_counts, right_side, panels, diag_leaf, diag_pair, diag_root)
    return solved.reshape(levels, 1, rhs, wide), updated


def solution(mesh):
    placed = (
        P("leaf", "row", None, None),
        P(None, "leaf", "row", None, None),
        P(None, "leaf", "row"),
        P("leaf", None, None),
        P(),
        P(),
        P(),
    )
    return jax.shard_map(
        functools.partial(on_device, GRIDS[mesh.shape["row"]], mesh.shape["leaf"]),
        mesh=mesh,
        in_specs=placed,
        out_specs=(P(None, "leaf", None, None), P("row", None, None)),
        check_vma=False,
    )
```

```python
import functools

import jax
import jax.numpy as jnp
from jax import lax
from jax.experimental import pallas as pl
from jax.experimental.pallas import tpu as pltpu
from jax.sharding import PartitionSpec as P

MESH = pl.DeviceIdType.MESH
F32, BF16 = jnp.float32, jnp.bfloat16
PAIRS = ((1, 2), (1, 3), (2, 3))
GRIDS = {64: (4, 8, 2), 8: (2, 2, 2)}
SEMS = 96


def meeting(level, n_leaf):
    return (1, 2, n_leaf, n_leaf)[level]


def kernel(grid, n_leaf, sup, cnt, rs_h, pan_h, dl_h, dp_h, dr_h, sol_o, upd_o, *scratch):
    ny, nz, nc = grid
    (rs, pan, dl, dp, dr, held, qacc, sol, base, xr, fin, slices, floods, pub, sem) = scratch
    levels, (tiles, wide, _) = len(pan), pan[0].shape
    rhs = rs.shape[1]
    low, mid, part = wide // ny, rhs // nc, rhs // nc // nz
    x, r = lax.axis_index("leaf"), lax.axis_index("row")
    y, z, c = r // (nz * nc), (r // nc) % nz, r % nc
    used = [0]
    drains = []

    def device(x_, y_, z_, c_):
        return (x_, (y_ * nz + z_) * nc + c_)

    def fresh():
        used[0] += 1
        assert used[0] <= SEMS
        return sem.at[used[0] - 1]

    def fetch(src, dst):
        copy = pltpu.make_async_copy(src, dst, fresh())
        copy.start()
        return copy

    def exchange(copies, whole):
        out, got = fresh(), fresh()
        for src, dst, dev in copies:
            pltpu.make_async_remote_copy(
                src_ref=src, dst_ref=dst, send_sem=out, recv_sem=got, device_id=dev, device_id_type=MESH
            ).start()
        drains.append(pltpu.make_async_copy(whole, whole, out))
        return pltpu.make_async_copy(whole, whole, got)

    def to_core(src, dst):
        return exchange([(src, dst, device(x, y, z, 1 - c))], dst)

    def scatter_z(src, dst):
        return exchange([(src.at[(z + k) % nz], dst.at[k - 1], device(x, y, (z + k) % nz, c)) for k in range(1, nz)], dst)

    def scatter_y(src, dst):
        return exchange([(src.at[(y + k) % ny], dst.at[k - 1], device(x, (y + k) % ny, z, c)) for k in range(1, ny)], dst)

    def gather_z(ref):
        return exchange(
            [(ref.at[z], ref.at[z], device(x, y, (z + k) % nz, c)) for k in range(1, nz)], ref.at[pl.ds(0, nz - 1)]
        )

    def total(mine, others):
        value = mine.astype(F32)
        for k in range(others.shape[0]):
            value = value + others[k].astype(F32)
        return value

    ready = {"rs": fetch(rs_h.at[0], rs), "d0": fetch(dl_h, dl)}
    for level, name in ((1, "p1"), (2, "p2"), (0, "p0"), (3, "p3")):
        ready[name] = fetch(pan_h.at[level, 0], pan[level])
    ready["d1"] = fetch(dp_h, dp)
    ready["d2"] = fetch(dr_h, dr)
    waited = set()

    def need(name):
        if name not in waited:
            waited.add(name)
            ready[name].wait()

    barrier = pltpu.get_barrier_semaphore()
    peers = [device(x, y, z, 1 - c)]
    peers += [device(x, y, (z + k) % nz, c) for k in range(1, nz)]
    peers += [device(x ^ i, (y + j) % ny, z, c) for i in range(n_leaf) for j in range(ny) if i or j]
    for dev in peers:
        pl.semaphore_signal(barrier, inc=1, device_id=dev, device_id_type=MESH)
    pl.semaphore_wait(barrier, len(peers))

    owner = [jnp.where(lax.div(sup[m], tiles) == r, 1.0, 0.0).astype(F32) for m in range(levels)]
    local = [lax.rem(sup[m], tiles) for m in range(levels)]
    columns = lax.broadcasted_iota(jnp.int32, (1, wide), 1)

    def product(level, tile, count):
        done = sol[level].reshape(rhs, wide)
        term = jnp.dot(done, pan[level][tile], preferred_element_type=F32)
        return jnp.where(columns < count, term, 0.0)

    def bulk(level):
        need(f"p{level}")

        def one(tile, carry):
            count = cnt[level, 0, tile]
            for m in range(level + 1):
                count = jnp.where(sup[m] == r * tiles + tile, 0, count)
            term = product(level, tile, count)
            before = rs[tile].astype(F32) if level == 0 else held[tile]
            held[tile] = before - term
            return carry

        lax.fori_loop(0, tiles, one, 0)

    def begin(m):
        qs, qr = slices[m][:2]
        rows = rs[local[m]].astype(F32)
        if m:
            rows = rows - qacc[m]
        rows = (rows * owner[m]).astype(BF16)
        for half in range(nc):
            qs[half] = rows[half * mid : (half + 1) * mid]
        return to_core(qs.at[1 - c], qr)

    def slice_z(m, arrival):
        qs, qr, zs, zr = slices[m][:4]
        arrival.wait()
        both = qs[c].astype(F32) + qr[...].astype(F32)
        zs[...] = both.astype(BF16).reshape(nz, part, wide)
        return scatter_z(zs, zr)

    def rows_of(m, arrival):
        zs, zr = slices[m][2:4]
        arrival.wait()
        return total(zs[z], zr).astype(BF16)

    def flood(m, value):
        n = meeting(m, n_leaf)
        cs, cr = floods[m]
        own = (x % n) * ny + y
        cs[...] = value
        cr[own] = value
        return exchange(
            [(cs, cr.at[own], device(x ^ a, (y + b) % ny, z, c)) for a in range(n) for b in range(ny) if a or b],
            cr.at[pl.ds(0, n * ny - 1)],
        )

    def solve(m, arrival):
        n = meeting(m, n_leaf)
        cr = floods[m][1]
        arrival.wait()
        if m < 2:
            merged = cr[0].astype(F32)
            for k in range(1, n * ny):
                merged = merged + cr[k].astype(F32)
            merged = merged.astype(BF16)
        else:
            parts = []
            for k in range(ny):
                value = cr[k]
                for a in range(1, n):
                    value = value + cr[a * ny + k]
                parts.append(value.astype(BF16))
            merged = jnp.concatenate(parts, axis=1)
        need(("d0", "d1", "d2", "d2")[m])
        inverse = dl[0] if m == 0 else dp[x // 2] if m == 1 else dr[m - 2]
        solved = jnp.dot(merged, inverse, preferred_element_type=F32).astype(BF16)
        sol[m, c, z] = solved
        return solved, gather_z(sol.at[m, c])

    def share(m, arrival):
        arrival.wait()
        return to_core(sol.at[m, c], sol.at[m, c])

    def keep(m, arrival):
        arrival.wait()
        drains.append(fetch(sol.at[m], sol_o.at[m]))

    pc, pcr, py, pyr, pz, pzr, pf = pub

    def publish_core():
        for i, (level, m) in enumerate(PAIRS):
            need(f"p{level}")
            live = jnp.where(columns < cnt[level, 0, local[m]], owner[m], 0.0).astype(BF16)
            tile = pan[level][local[m]] * live
            for half in range(nc):
                pc[half, i] = tile[half * (wide // nc) : (half + 1) * (wide // nc)]
        return to_core(pc.at[1 - c], pcr)

    def publish_columns(arrival):
        arrival.wait()
        for i in range(len(PAIRS)):
            both = (pc[c, i].astype(F32) + pcr[i].astype(F32)).astype(BF16)
            for k in range(ny):
                py[k, i] = both[:, k * low : (k + 1) * low]

    def publish_z(arrival):
        arrival.wait()
        step = wide // nc // nz
        for i in range(len(PAIRS)):
            value = py[y, i].astype(F32)
            for k in range(ny - 1):
                value = value + pyr[k, i].astype(F32)
            value = value.astype(BF16)
            for k in range(nz):
                pz[k, i] = value[k * step : (k + 1) * step]
        return scatter_z(pz, pzr)

    def publish_gather(arrival):
        arrival.wait()
        pf[c, z] = total(pz[z], pzr).astype(BF16)
        return gather_z(pf.at[c])

    def coupling(level, m):
        return pf[:, :, PAIRS.index((level, m))].reshape(wide, low)

    need("rs")
    arrival = slice_z(0, begin(0))
    publish_columns(publish_core())
    arrival = flood(0, rows_of(0, arrival))
    published = scatter_y(py, pyr)
    _, arrival = solve(0, arrival)
    published = publish_z(published)
    keep(0, share(0, arrival))
    need("p0")
    arrivals = {}
    for m in (1, 2, 3):
        qacc[m] = product(0, local[m], cnt[0, 0, local[m]])
        arrivals[m] = begin(m)
    for m in (1, 2, 3):
        arrivals[m] = slice_z(m, arrivals[m])
    published = publish_gather(published)
    bulk(0)
    merge1 = flood(1, rows_of(1, arrivals[1]))
    for m in (2, 3):
        rows = rows_of(m, arrivals[m])
        ys, yr = slices[m][4:]
        for k in range(ny):
            ys[k] = rows[:, k * low : (k + 1) * low]
        arrivals[m] = scatter_y(ys, yr)
    published.wait()
    published = to_core(pf.at[c], pf.at[c])
    solved1, spread1 = solve(1, merge1)
    published.wait()
    arrivals[2].wait()
    piece = total(slices[2][4][y], slices[2][5])
    merge2 = flood(2, piece - jnp.dot(solved1, coupling(1, 2), preferred_element_type=F32))
    arrivals[3].wait()
    piece = total(slices[3][4][y], slices[3][5])
    piece = piece - jnp.dot(solved1, coupling(1, 3), preferred_element_type=F32)
    spread1 = share(1, spread1)
    solved2, spread2 = solve(2, merge2)
    merge3 = flood(3, piece - jnp.dot(solved2, coupling(2, 3), preferred_element_type=F32))
    keep(1, spread1)
    bulk(1)
    spread2 = share(2, spread2)
    _, spread3 = solve(3, merge3)
    keep(2, spread2)
    bulk(2)
    keep(3, share(3, spread3))
    bulk(3)
    for tile in range(tiles):
        base[tile] = held[tile].astype(BF16)
    exchange([(base.at[x ^ k], xr.at[k - 1], device(x ^ k, y, z, c)) for k in range(1, n_leaf)], xr).wait()
    fin[...] = total(held[x], xr).astype(BF16)
    arrival = exchange(
        [(fin, upd_o.at[x], device(x ^ k, y, z, c)) for k in range(1, n_leaf)], upd_o.at[pl.ds(0, n_leaf - 1)]
    )
    drains.append(fetch(fin, upd_o.at[x]))
    arrival.wait()
    for copy in drains:
        copy.wait()


def on_device(grid, n_leaf, right_side, panels, tile_counts, diag_leaf, diag_pair, diag_root, sup_rows):
    ny, nz, nc = grid
    levels, _, tiles, wide, _ = panels.shape
    rhs = right_side.shape[2]
    mid, part, low = rhs // nc, rhs // nc // nz, wide // ny
    pairs, step = len(PAIRS), wide // nc // nz
    slices, floods = [], []
    for m in range(levels):
        slices.append(
            [
                pltpu.VMEM((nc, mid, wide), BF16),
                pltpu.VMEM((mid, wide), BF16),
                pltpu.VMEM((nz, part, wide), BF16),
                pltpu.VMEM((nz - 1, part, wide), BF16),
            ]
        )
        if m > 1:
            slices[m] += [pltpu.VMEM((ny, part, low), BF16), pltpu.VMEM((ny - 1, part, low), BF16)]
        piece, kind = ((part, wide), BF16) if m < 2 else ((part, low), F32)
        floods.append([pltpu.VMEM(piece, kind), pltpu.VMEM((meeting(m, n_leaf) * ny, *piece), kind)])
    pub = [
        pltpu.VMEM((nc, pairs, wide // nc, wide), BF16),
        pltpu.VMEM((pairs, wide // nc, wide), BF16),
        pltpu.VMEM((ny, pairs, wide // nc, low), BF16),
        pltpu.VMEM((ny - 1, pairs, wide // nc, low), BF16),
        pltpu.VMEM((nz, pairs, step, low), BF16),
        pltpu.VMEM((nz - 1, pairs, step, low), BF16),
        pltpu.VMEM((nc, nz, pairs, step, low), BF16),
    ]
    scratch = [
        pltpu.VMEM((tiles, rhs, wide), BF16),
        [pltpu.VMEM((tiles, wide, wide), BF16)] * levels,
        pltpu.VMEM((1, wide, wide), BF16),
        pltpu.VMEM((2, wide, wide), BF16),
        pltpu.VMEM((2, wide, wide), BF16),
        pltpu.VMEM((tiles, rhs, wide), F32),
        pltpu.VMEM((levels, rhs, wide), F32),
        pltpu.VMEM((levels, nc, nz, part, wide), BF16),
        pltpu.VMEM((tiles, rhs, wide), BF16),
        pltpu.VMEM((n_leaf - 1, rhs, wide), BF16),
        pltpu.VMEM((rhs, wide), BF16),
        slices,
        floods,
        pub,
        pltpu.SemaphoreType.DMA((SEMS,)),
    ]
    anywhere, scalars = pl.BlockSpec(memory_space=pl.ANY), pl.BlockSpec(memory_space=pltpu.SMEM)
    solved, updated = pl.pallas_call(
        functools.partial(kernel, grid, n_leaf),
        out_shape=(
            jax.ShapeDtypeStruct((levels, nc, nz, part, wide), BF16),
            jax.ShapeDtypeStruct((tiles, rhs, wide), BF16),
        ),
        in_specs=[scalars, scalars] + [anywhere] * 5,
        out_specs=(anywhere, anywhere),
        scratch_shapes=scratch,
        compiler_params=pltpu.CompilerParams(
            collective_id=0, has_side_effects=True, vmem_limit_bytes=56 * 2**20
        ),
    )(sup_rows, tile_counts, right_side, panels, diag_leaf, diag_pair, diag_root)
    return solved.reshape(levels, 1, rhs, wide), updated


def solution(mesh):
    placed = (
        P("leaf", "row", None, None),
        P(None, "leaf", "row", None, None),
        P(None, "leaf", "row"),
        P("leaf", None, None),
        P(),
        P(),
        P(),
    )
    return jax.shard_map(
        functools.partial(on_device, GRIDS[mesh.shape["row"]], mesh.shape["leaf"]),
        mesh=mesh,
        in_specs=placed,
        out_specs=(P(None, "leaf", None, None), P("row", None, None)),
        check_vma=False,
    )
```

```python
import functools

import jax
import jax.numpy as jnp
from jax import lax
from jax.experimental import pallas as pl
from jax.experimental.pallas import tpu as pltpu
from jax.sharding import PartitionSpec as P

MESH = pl.DeviceIdType.MESH
F32, BF16 = jnp.float32, jnp.bfloat16
PAIRS = ((1, 2), (1, 3), (2, 3))
GRIDS = {64: (4, 8, 2), 8: (2, 2, 2)}
SEMS = 128


def meeting(level, n_leaf):
    return (1, 2, n_leaf, n_leaf)[level]


def kernel(grid, n_leaf, sup, cnt, rs_h, pan_h, dl_h, dp_h, dr_h, sol_o, upd_o, *scratch):
    ny, nz, nc = grid
    (rs, pan, dl, dp, dr, held, qacc, sol, live, sums, acc, upd, folds, slices, floods, pub, sem) = scratch
    levels, (tiles, wide, _) = len(pan), pan[0].shape
    rhs = rs.shape[1]
    low, mid, part = wide // ny, rhs // nc, rhs // nc // nz
    x, r = lax.axis_index("leaf"), lax.axis_index("row")
    y, z, c = r // (nz * nc), (r // nc) % nz, r % nc
    used = [0]
    drains = []

    def device(x_, y_, z_, c_):
        return (x_, (y_ * nz + z_) * nc + c_)

    def fresh():
        used[0] += 1
        assert used[0] <= SEMS
        return sem.at[used[0] - 1]

    def fetch(src, dst):
        copy = pltpu.make_async_copy(src, dst, fresh())
        copy.start()
        return copy

    def exchange(copies, whole):
        out, got = fresh(), fresh()
        for src, dst, dev in copies:
            pltpu.make_async_remote_copy(
                src_ref=src, dst_ref=dst, send_sem=out, recv_sem=got, device_id=dev, device_id_type=MESH
            ).start()
        drains.append(pltpu.make_async_copy(whole, whole, out))
        return pltpu.make_async_copy(whole, whole, got)

    def to_core(src, dst):
        return exchange([(src, dst, device(x, y, z, 1 - c))], dst)

    def scatter_z(src, dst):
        return exchange([(src.at[(z + k) % nz], dst.at[k - 1], device(x, y, (z + k) % nz, c)) for k in range(1, nz)], dst)

    def scatter_y(src, dst):
        return exchange([(src.at[(y + k) % ny], dst.at[k - 1], device(x, (y + k) % ny, z, c)) for k in range(1, ny)], dst)

    def gather_z(ref):
        return exchange(
            [(ref.at[z], ref.at[z], device(x, y, (z + k) % nz, c)) for k in range(1, nz)], ref.at[pl.ds(0, nz - 1)]
        )

    def total(mine, others):
        value = mine.astype(F32)
        for k in range(others.shape[0]):
            value = value + others[k].astype(F32)
        return value

    ready = {"rs": fetch(rs_h.at[0], rs), "d0": fetch(dl_h, dl)}
    for level, name in ((1, "p1"), (2, "p2"), (3, "p3"), (0, "p0")):
        ready[name] = fetch(pan_h.at[level, 0], pan[level])
    ready["d1"] = fetch(dp_h, dp)
    ready["d2"] = fetch(dr_h, dr)
    waited = set()

    def need(name):
        if name not in waited:
            waited.add(name)
            ready[name].wait()

    barrier = pltpu.get_barrier_semaphore()
    peers = [device(x, y, z, 1 - c)]
    peers += [device(x, y, (z + k) % nz, c) for k in range(1, nz)]
    peers += [device(x ^ i, (y + j) % ny, z, c) for i in range(n_leaf) for j in range(ny) if i or j]
    for dev in peers:
        pl.semaphore_signal(barrier, inc=1, device_id=dev, device_id_type=MESH)
    pl.semaphore_wait(barrier, len(peers))

    owner = [jnp.where(lax.div(sup[m], tiles) == r, 1.0, 0.0).astype(F32) for m in range(levels)]
    local = [lax.rem(sup[m], tiles) for m in range(levels)]
    columns = lax.broadcasted_iota(jnp.int32, (1, wide), 1)

    def product(level, tile, count):
        done = sol[level].reshape(rhs, wide)
        term = jnp.dot(done, pan[level][tile], preferred_element_type=F32)
        return jnp.where(columns < count, term, 0.0)

    def bulk(level):
        need(f"p{level}")

        def one(tile, carry):
            count = cnt[level, 0, tile]
            for m in range(level + 1):
                count = jnp.where(sup[m] == r * tiles + tile, 0, count)
            term = product(level, tile, count)
            before = rs[tile].astype(F32) if level == 0 else held[tile]
            held[tile] = before - term
            return carry

        lax.fori_loop(0, tiles, one, 0)

    def begin(m):
        qs, qr = slices[m][:2]
        rows = rs[local[m]].astype(F32)
        if m:
            rows = rows - qacc[m]
        rows = (rows * owner[m]).astype(BF16)
        for half in range(nc):
            qs[half] = rows[half * mid : (half + 1) * mid]
        return to_core(qs.at[1 - c], qr)

    def slice_z(m, arrival):
        qs, qr, zs, zr = slices[m][:4]
        arrival.wait()
        both = qs[c].astype(F32) + qr[...].astype(F32)
        zs[...] = both.astype(BF16).reshape(nz, part, wide)
        return scatter_z(zs, zr)

    def rows_of(m, arrival):
        zs, zr = slices[m][2:4]
        arrival.wait()
        return total(zs[z], zr).astype(BF16)

    def flood(m, value):
        n = meeting(m, n_leaf)
        cs, cr = floods[m]
        own = (x % n) * ny + y
        cs[...] = value
        cr[own] = value
        return exchange(
            [(cs, cr.at[own], device(x ^ a, (y + b) % ny, z, c)) for a in range(n) for b in range(ny) if a or b],
            cr.at[pl.ds(0, n * ny - 1)],
        )

    def solve(m, arrival):
        n = meeting(m, n_leaf)
        cr = floods[m][1]
        arrival.wait()
        if m < 2:
            merged = cr[0].astype(F32)
            for k in range(1, n * ny):
                merged = merged + cr[k].astype(F32)
            merged = merged.astype(BF16)
        else:
            parts = []
            for k in range(ny):
                value = cr[k]
                for a in range(1, n):
                    value = value + cr[a * ny + k]
                parts.append(value.astype(BF16))
            merged = jnp.concatenate(parts, axis=1)
        need(("d0", "d1", "d2", "d2")[m])
        inverse = dl[0] if m == 0 else dp[x // 2] if m == 1 else dr[m - 2]
        solved = jnp.dot(merged, inverse, preferred_element_type=F32).astype(BF16)
        sol[m, c, z] = solved
        return solved, gather_z(sol.at[m, c])

    def share(m, arrival):
        arrival.wait()
        return to_core(sol.at[m, c], sol.at[m, c])

    def keep(m, arrival):
        arrival.wait()
        drains.append(fetch(sol.at[m], sol_o.at[m]))

    pc, pcr, py, pyr, pz, pzr, pf = pub

    def publish_core():
        for i, (level, m) in enumerate(PAIRS):
            need(f"p{level}")
            live = jnp.where(columns < cnt[level, 0, local[m]], owner[m], 0.0).astype(BF16)
            tile = pan[level][local[m]] * live
            for half in range(nc):
                pc[half, i] = tile[half * (wide // nc) : (half + 1) * (wide // nc)]
        return to_core(pc.at[1 - c], pcr)

    def publish_columns(arrival):
        arrival.wait()
        for i in range(len(PAIRS)):
            both = (pc[c, i].astype(F32) + pcr[i].astype(F32)).astype(BF16)
            for k in range(ny):
                py[k, i] = both[:, k * low : (k + 1) * low]

    def publish_z(arrival):
        arrival.wait()
        step = wide // nc // nz
        for i in range(len(PAIRS)):
            value = py[y, i].astype(F32)
            for k in range(ny - 1):
                value = value + pyr[k, i].astype(F32)
            value = value.astype(BF16)
            for k in range(nz):
                pz[k, i] = value[k * step : (k + 1) * step]
        return scatter_z(pz, pzr)

    def publish_gather(arrival):
        arrival.wait()
        pf[c, z] = total(pz[z], pzr).astype(BF16)
        return gather_z(pf.at[c])

    def coupling(level, m):
        return pf[:, :, PAIRS.index((level, m))].reshape(wide, low)

    def after(k):
        return (x + k) % n_leaf

    def fold(src, bufs):
        relay, near = bufs[:2]
        half = relay.shape[1]
        first, second = pl.ds(0, half), pl.ds(half, half)
        up, down = device(after(1), y, z, c), device(after(n_leaf - 1), y, z, c)
        far = after(2)
        relayed = exchange([(src.at[far, first], relay.at[0], up), (src.at[far, second], relay.at[1], down)], relay)
        direct = exchange(
            [(src.at[after(1), second], near.at[1], up), (src.at[after(n_leaf - 1), first], near.at[0], down)], near
        )
        return relayed, direct

    def fold_on(src, bufs, relayed):
        relay, _, out, last = bufs
        half = relay.shape[1]
        up, down = device(after(1), y, z, c), device(after(n_leaf - 1), y, z, c)
        relayed.wait()
        out[0] = (src[after(1), :half].astype(F32) + relay[0].astype(F32)).astype(BF16)
        out[1] = (src[after(n_leaf - 1), half:].astype(F32) + relay[1].astype(F32)).astype(BF16)
        return exchange([(out.at[0], last.at[0], up), (out.at[1], last.at[1], down)], last)

    def folded(mine, bufs, i):
        _, near, _, last = bufs
        half = near.shape[1]
        return mine[i * half : (i + 1) * half].astype(F32) + near[i].astype(F32) + last[i].astype(F32)

    def mask_tiles(level):
        need(f"p{level}")
        into = live[level - 2]

        def one(tile, carry):
            count = cnt[level, 0, tile]
            for m in range(level + 1):
                count = jnp.where(sup[m] == r * tiles + tile, 0, count)
            into[tile] = pan[level][tile] * jnp.where(columns < count, 1.0, 0.0).astype(BF16)
            return carry

        lax.fori_loop(0, tiles, one, 0)

    def sum_tiles(level, arrivals):
        for arrival in arrivals:
            arrival.wait()
        half = wide // 2
        for i in range(2):
            sums[level - 2, i * half : (i + 1) * half] = folded(live[level - 2][x], folds[level - 2], i).astype(BF16)

    def take(level):
        acc[...] = acc[...] - jnp.dot(sol[level].reshape(rhs, wide), sums[level - 2], preferred_element_type=F32)

    need("rs")
    arrival = slice_z(0, begin(0))
    published = publish_core()
    mask_tiles(3)
    relayed3, direct3 = fold(live[1], folds[1])
    publish_columns(published)
    arrival = flood(0, rows_of(0, arrival))
    published = scatter_y(py, pyr)
    mask_tiles(2)
    _, arrival = solve(0, arrival)
    last3 = fold_on(live[1], folds[1], relayed3)
    published = publish_z(published)
    relayed2, direct2 = fold(live[0], folds[0])
    shared = share(0, arrival)
    keep(0, shared)
    need("p0")
    arrivals = {}
    for m in (1, 2):
        qacc[m] = product(0, local[m], cnt[0, 0, local[m]])
        arrivals[m] = begin(m)
    arrivals[1] = slice_z(1, arrivals[1])
    published = publish_gather(published)
    qacc[3] = product(0, local[3], cnt[0, 0, local[3]])
    arrivals[3] = begin(3)
    for m in (2, 3):
        arrivals[m] = slice_z(m, arrivals[m])
    merge1 = flood(1, rows_of(1, arrivals[1]))
    bulk(0)
    last2 = fold_on(live[0], folds[0], relayed2)
    for m in (2, 3):
        rows = rows_of(m, arrivals[m])
        ys, yr = slices[m][4:]
        for k in range(ny):
            ys[k] = rows[:, k * low : (k + 1) * low]
        arrivals[m] = scatter_y(ys, yr)
    published.wait()
    published = to_core(pf.at[c], pf.at[c])
    solved1, spread1 = solve(1, merge1)
    published.wait()
    arrivals[2].wait()
    piece = total(slices[2][4][y], slices[2][5])
    merge2 = flood(2, piece - jnp.dot(solved1, coupling(1, 2), preferred_element_type=F32))
    arrivals[3].wait()
    piece = total(slices[3][4][y], slices[3][5])
    piece = piece - jnp.dot(solved1, coupling(1, 3), preferred_element_type=F32)
    sum_tiles(3, (direct3, last3))
    solved2, spread2 = solve(2, merge2)
    merge3 = flood(3, piece - jnp.dot(solved2, coupling(2, 3), preferred_element_type=F32))
    keep(1, share(1, spread1))
    bulk(1)
    for tile in range(tiles):
        upd[tile] = held[tile].astype(BF16)
    relayed, direct = fold(upd, folds[2])
    _, spread3 = solve(3, merge3)
    shared = share(2, spread2)
    sum_tiles(2, (direct2, last2))
    keep(2, shared)
    last = fold_on(upd, folds[2], relayed)
    shared = share(3, spread3)
    direct.wait()
    last.wait()
    half = rhs // 2
    for i in range(2):
        acc[i * half : (i + 1) * half] = folded(held[x], folds[2], i)
    take(2)
    keep(3, shared)
    take(3)
    fin, got = folds[3]
    for i in range(2):
        fin[i] = acc[i * half : (i + 1) * half].astype(BF16)
    up, down = device(after(1), y, z, c), device(after(n_leaf - 1), y, z, c)
    ahead = exchange([(fin.at[0], got.at[0, 0], up), (fin.at[1], got.at[1, 1], down)], fin)
    behind = exchange([(fin.at[1], got.at[0, 1], up), (fin.at[0], got.at[1, 0], down)], fin)
    for i in range(2):
        drains.append(fetch(fin.at[i], upd_o.at[x, pl.ds(i * half, half)]))
    ahead.wait()
    passed = exchange([(got.at[0, 0], got.at[2, 0], up), (got.at[1, 1], got.at[2, 1], down)], fin)
    behind.wait()
    for k, origin in ((0, after(n_leaf - 1)), (1, after(1))):
        for i in range(2):
            drains.append(fetch(got.at[k, i], upd_o.at[origin, pl.ds(i * half, half)]))
    passed.wait()
    for i in range(2):
        drains.append(fetch(got.at[2, i], upd_o.at[after(2), pl.ds(i * half, half)]))
    for copy in drains:
        copy.wait()


def on_device(grid, n_leaf, right_side, panels, tile_counts, diag_leaf, diag_pair, diag_root, sup_rows):
    ny, nz, nc = grid
    levels, _, tiles, wide, _ = panels.shape
    rhs = right_side.shape[2]
    mid, part, low = rhs // nc, rhs // nc // nz, wide // ny
    pairs, step = len(PAIRS), wide // nc // nz
    slices, floods = [], []
    for m in range(levels):
        slices.append(
            [
                pltpu.VMEM((nc, mid, wide), BF16),
                pltpu.VMEM((mid, wide), BF16),
                pltpu.VMEM((nz, part, wide), BF16),
                pltpu.VMEM((nz - 1, part, wide), BF16),
            ]
        )
        if m > 1:
            slices[m] += [pltpu.VMEM((ny, part, low), BF16), pltpu.VMEM((ny - 1, part, low), BF16)]
        piece, kind = ((part, wide), BF16) if m < 2 else ((part, low), F32)
        floods.append([pltpu.VMEM(piece, kind), pltpu.VMEM((meeting(m, n_leaf) * ny, *piece), kind)])
    pub = [
        pltpu.VMEM((nc, pairs, wide // nc, wide), BF16),
        pltpu.VMEM((pairs, wide // nc, wide), BF16),
        pltpu.VMEM((ny, pairs, wide // nc, low), BF16),
        pltpu.VMEM((ny - 1, pairs, wide // nc, low), BF16),
        pltpu.VMEM((nz, pairs, step, low), BF16),
        pltpu.VMEM((nz - 1, pairs, step, low), BF16),
        pltpu.VMEM((nc, nz, pairs, step, low), BF16),
    ]
    scratch = [
        pltpu.VMEM((tiles, rhs, wide), BF16),
        [pltpu.VMEM((tiles, wide, wide), BF16)] * levels,
        pltpu.VMEM((1, wide, wide), BF16),
        pltpu.VMEM((2, wide, wide), BF16),
        pltpu.VMEM((2, wide, wide), BF16),
        pltpu.VMEM((tiles, rhs, wide), F32),
        pltpu.VMEM((levels, rhs, wide), F32),
        pltpu.VMEM((levels, nc, nz, part, wide), BF16),
        [pltpu.VMEM((tiles, wide, wide), BF16)] * 2,
        pltpu.VMEM((2, wide, wide), BF16),
        pltpu.VMEM((rhs, wide), F32),
        pltpu.VMEM((tiles, rhs, wide), BF16),
        [[pltpu.VMEM((2, length // 2, wide), BF16)] * 4 for length in (wide, wide, rhs)]
        + [[pltpu.VMEM((2, rhs // 2, wide), BF16), pltpu.VMEM((n_leaf - 1, 2, rhs // 2, wide), BF16)]],
        slices,
        floods,
        pub,
        pltpu.SemaphoreType.DMA((SEMS,)),
    ]
    anywhere, scalars = pl.BlockSpec(memory_space=pl.ANY), pl.BlockSpec(memory_space=pltpu.SMEM)
    solved, updated = pl.pallas_call(
        functools.partial(kernel, grid, n_leaf),
        out_shape=(
            jax.ShapeDtypeStruct((levels, nc, nz, part, wide), BF16),
            jax.ShapeDtypeStruct((tiles, rhs, wide), BF16),
        ),
        in_specs=[scalars, scalars] + [anywhere] * 5,
        out_specs=(anywhere, anywhere),
        scratch_shapes=scratch,
        compiler_params=pltpu.CompilerParams(
            collective_id=0, has_side_effects=True, vmem_limit_bytes=56 * 2**20
        ),
    )(sup_rows, tile_counts, right_side, panels, diag_leaf, diag_pair, diag_root)
    return solved.reshape(levels, 1, rhs, wide), updated


def solution(mesh):
    placed = (
        P("leaf", "row", None, None),
        P(None, "leaf", "row", None, None),
        P(None, "leaf", "row"),
        P("leaf", None, None),
        P(),
        P(),
        P(),
    )
    return jax.shard_map(
        functools.partial(on_device, GRIDS[mesh.shape["row"]], mesh.shape["leaf"]),
        mesh=mesh,
        in_specs=placed,
        out_specs=(P(None, "leaf", None, None), P("row", None, None)),
        check_vma=False,
    )
```

```python
import functools

import jax
import jax.numpy as jnp
from jax import lax
from jax.experimental import pallas as pl
from jax.experimental.pallas import tpu as pltpu
from jax.sharding import PartitionSpec as P

MESH = pl.DeviceIdType.MESH
F32, BF16 = jnp.float32, jnp.bfloat16
BATCHES = (((1, 2),), ((1, 3), (2, 3)))
GRIDS = {64: (4, 8, 2), 8: (2, 2, 2)}
SEMS = 128


def meeting(level, n_leaf):
    return (1, 2, n_leaf, n_leaf)[level]


def kernel(grid, n_leaf, sup, cnt, rs_h, pan_h, dl_h, dp_h, dr_h, sol_o, upd_o, *scratch):
    ny, nz, nc = grid
    (rs, pan, dl, dp, dr, held, qacc, sol, live, sums, acc, upd, folds, slices, floods, pub, sem) = scratch
    levels, (tiles, wide, _) = len(pan), pan[0].shape
    rhs = rs.shape[1]
    low, mid, part = wide // ny, rhs // nc, rhs // nc // nz
    x, r = lax.axis_index("leaf"), lax.axis_index("row")
    y, z, c = r // (nz * nc), (r // nc) % nz, r % nc
    used = [0]
    drains = []

    def device(x_, y_, z_, c_):
        return (x_, (y_ * nz + z_) * nc + c_)

    def fresh():
        used[0] += 1
        assert used[0] <= SEMS
        return sem.at[used[0] - 1]

    def fetch(src, dst):
        copy = pltpu.make_async_copy(src, dst, fresh())
        copy.start()
        return copy

    def exchange(copies, whole):
        out, got = fresh(), fresh()
        for src, dst, dev in copies:
            pltpu.make_async_remote_copy(
                src_ref=src, dst_ref=dst, send_sem=out, recv_sem=got, device_id=dev, device_id_type=MESH
            ).start()
        drains.append(pltpu.make_async_copy(whole, whole, out))
        return pltpu.make_async_copy(whole, whole, got)

    def to_core(src, dst):
        return exchange([(src, dst, device(x, y, z, 1 - c))], dst)

    def scatter_z(src, dst):
        return exchange([(src.at[(z + k) % nz], dst.at[k - 1], device(x, y, (z + k) % nz, c)) for k in range(1, nz)], dst)

    def scatter_y(src, dst):
        return exchange([(src.at[(y + k) % ny], dst.at[k - 1], device(x, (y + k) % ny, z, c)) for k in range(1, ny)], dst)

    def gather_z(ref):
        return exchange(
            [(ref.at[z], ref.at[z], device(x, y, (z + k) % nz, c)) for k in range(1, nz)], ref.at[pl.ds(0, nz - 1)]
        )

    def total(mine, others):
        value = mine.astype(F32)
        for k in range(others.shape[0]):
            value = value + others[k].astype(F32)
        return value

    ready = {"rs": fetch(rs_h.at[0], rs), "d0": fetch(dl_h, dl)}
    for level, name in ((1, "p1"), (2, "p2"), (3, "p3"), (0, "p0")):
        ready[name] = fetch(pan_h.at[level, 0], pan[level])
    ready["d1"] = fetch(dp_h, dp)
    ready["d2"] = fetch(dr_h, dr)
    waited = set()

    def need(name):
        if name not in waited:
            waited.add(name)
            ready[name].wait()

    barrier = pltpu.get_barrier_semaphore()
    peers = [device(x, y, z, 1 - c)]
    peers += [device(x, y, (z + k) % nz, c) for k in range(1, nz)]
    peers += [device(x ^ i, (y + j) % ny, z, c) for i in range(n_leaf) for j in range(ny) if i or j]
    for dev in peers:
        pl.semaphore_signal(barrier, inc=1, device_id=dev, device_id_type=MESH)
    pl.semaphore_wait(barrier, len(peers))

    owner = [jnp.where(lax.div(sup[m], tiles) == r, 1.0, 0.0).astype(F32) for m in range(levels)]
    local = [lax.rem(sup[m], tiles) for m in range(levels)]
    columns = lax.broadcasted_iota(jnp.int32, (1, wide), 1)

    def product(level, tile, count):
        done = sol[level].reshape(rhs, wide)
        term = jnp.dot(done, pan[level][tile], preferred_element_type=F32)
        return jnp.where(columns < count, term, 0.0)

    def bulk(level):
        need(f"p{level}")

        def one(tile, carry):
            count = cnt[level, 0, tile]
            for m in range(level + 1):
                count = jnp.where(sup[m] == r * tiles + tile, 0, count)
            term = product(level, tile, count)
            before = rs[tile].astype(F32) if level == 0 else held[tile]
            held[tile] = before - term
            return carry

        lax.fori_loop(0, tiles, one, 0)

    def begin(m):
        qs, qr = slices[m][:2]
        rows = rs[local[m]].astype(F32)
        if m:
            rows = rows - qacc[m]
        rows = (rows * owner[m]).astype(BF16)
        for half in range(nc):
            qs[half] = rows[half * mid : (half + 1) * mid]
        return to_core(qs.at[1 - c], qr)

    def slice_z(m, arrival):
        qs, qr, zs, zr = slices[m][:4]
        arrival.wait()
        both = qs[c].astype(F32) + qr[...].astype(F32)
        zs[...] = both.astype(BF16).reshape(nz, part, wide)
        return scatter_z(zs, zr)

    def rows_of(m, arrival):
        zs, zr = slices[m][2:4]
        arrival.wait()
        return total(zs[z], zr).astype(BF16)

    def flood(m, value):
        n = meeting(m, n_leaf)
        cs, cr = floods[m]
        own = (x % n) * ny + y
        cs[...] = value
        cr[own] = value
        return exchange(
            [(cs, cr.at[own], device(x ^ a, (y + b) % ny, z, c)) for a in range(n) for b in range(ny) if a or b],
            cr.at[pl.ds(0, n * ny - 1)],
        )

    def solve(m, arrival):
        n = meeting(m, n_leaf)
        cr = floods[m][1]
        arrival.wait()
        if m < 2:
            merged = cr[0].astype(F32)
            for k in range(1, n * ny):
                merged = merged + cr[k].astype(F32)
            merged = merged.astype(BF16)
        else:
            parts = []
            for k in range(ny):
                value = cr[k]
                for a in range(1, n):
                    value = value + cr[a * ny + k]
                parts.append(value.astype(BF16))
            merged = jnp.concatenate(parts, axis=1)
        need(("d0", "d1", "d2", "d2")[m])
        inverse = dl[0] if m == 0 else dp[x // 2] if m == 1 else dr[m - 2]
        solved = jnp.dot(merged, inverse, preferred_element_type=F32).astype(BF16)
        sol[m, c, z] = solved
        return solved, gather_z(sol.at[m, c])

    def share(m, arrival):
        arrival.wait()
        return to_core(sol.at[m, c], sol.at[m, c])

    def keep(m, arrival):
        arrival.wait()
        drains.append(fetch(sol.at[m], sol_o.at[m]))

    def publish_core(batch):
        pc, pcr = pub[batch][:2]
        for i, (level, m) in enumerate(BATCHES[batch]):
            need(f"p{level}")
            alive = jnp.where(columns < cnt[level, 0, local[m]], owner[m], 0.0).astype(BF16)
            tile = pan[level][local[m]] * alive
            for half in range(nc):
                pc[half, i] = tile[half * (wide // nc) : (half + 1) * (wide // nc)]
        return to_core(pc.at[1 - c], pcr)

    def publish_y(batch, arrival):
        pc, pcr, py, pyr = pub[batch][:4]
        arrival.wait()
        for i in range(len(BATCHES[batch])):
            both = (pc[c, i].astype(F32) + pcr[i].astype(F32)).astype(BF16)
            for k in range(ny):
                py[k, i] = both[:, k * low : (k + 1) * low]
        return scatter_y(py, pyr)

    def publish_z(batch, arrival):
        py, pyr, pz, pzr = pub[batch][2:6]
        arrival.wait()
        step = wide // nc // nz
        for i in range(len(BATCHES[batch])):
            value = py[y, i].astype(F32)
            for k in range(ny - 1):
                value = value + pyr[k, i].astype(F32)
            value = value.astype(BF16)
            for k in range(nz):
                pz[k, i] = value[k * step : (k + 1) * step]
        return scatter_z(pz, pzr)

    def publish_gather(batch, arrival):
        pz, pzr, pf = pub[batch][4:]
        arrival.wait()
        pf[c, z] = total(pz[z], pzr).astype(BF16)
        return gather_z(pf.at[c])

    def publish_last(batch, arrival):
        pf = pub[batch][6]
        arrival.wait()
        return to_core(pf.at[c], pf.at[c])

    def coupling(level, m):
        batch = 0 if (level, m) in BATCHES[0] else 1
        return pub[batch][6][:, :, BATCHES[batch].index((level, m))].reshape(wide, low)

    def after(k):
        return (x + k) % n_leaf

    def fold(src, bufs):
        relay, near = bufs[:2]
        half = relay.shape[1]
        first, second = pl.ds(0, half), pl.ds(half, half)
        up, down = device(after(1), y, z, c), device(after(n_leaf - 1), y, z, c)
        far = after(2)
        relayed = exchange([(src.at[far, first], relay.at[0], up), (src.at[far, second], relay.at[1], down)], relay)
        direct = exchange(
            [(src.at[after(1), second], near.at[1], up), (src.at[after(n_leaf - 1), first], near.at[0], down)], near
        )
        return relayed, direct

    def fold_on(src, bufs, relayed):
        relay, _, out, last = bufs
        half = relay.shape[1]
        up, down = device(after(1), y, z, c), device(after(n_leaf - 1), y, z, c)
        relayed.wait()
        out[0] = (src[after(1), :half].astype(F32) + relay[0].astype(F32)).astype(BF16)
        out[1] = (src[after(n_leaf - 1), half:].astype(F32) + relay[1].astype(F32)).astype(BF16)
        return exchange([(out.at[0], last.at[0], up), (out.at[1], last.at[1], down)], last)

    def folded(mine, bufs, i):
        _, near, _, last = bufs
        half = near.shape[1]
        return mine[i * half : (i + 1) * half].astype(F32) + near[i].astype(F32) + last[i].astype(F32)

    def mask_tiles(level):
        need(f"p{level}")
        into = live[level - 2]

        def one(tile, carry):
            count = cnt[level, 0, tile]
            for m in range(level + 1):
                count = jnp.where(sup[m] == r * tiles + tile, 0, count)
            into[tile] = pan[level][tile] * jnp.where(columns < count, 1.0, 0.0).astype(BF16)
            return carry

        lax.fori_loop(0, tiles, one, 0)

    def sum_tiles(level, arrivals):
        for arrival in arrivals:
            arrival.wait()
        half = wide // 2
        for i in range(2):
            sums[level - 2, i * half : (i + 1) * half] = folded(live[level - 2][x], folds[level - 2], i).astype(BF16)

    def take(level, half):
        done = sol[level, half].reshape(mid, wide)
        return acc[half] - jnp.dot(done, sums[level - 2], preferred_element_type=F32)

    need("rs")
    arrival = slice_z(0, begin(0))
    pub_a = publish_core(0)
    pub_b = publish_core(1)
    mask_tiles(3)
    relayed3, direct3 = fold(live[1], folds[1])
    arrival = flood(0, rows_of(0, arrival))
    pub_a = publish_y(0, pub_a)
    pub_b = publish_y(1, pub_b)
    mask_tiles(2)
    _, arrival = solve(0, arrival)
    pub_a = publish_z(0, pub_a)
    last3 = fold_on(live[1], folds[1], relayed3)
    relayed2, direct2 = fold(live[0], folds[0])
    keep(0, share(0, arrival))
    need("p0")
    arrivals = {}
    for m in (1, 2):
        qacc[m] = product(0, local[m], cnt[0, 0, local[m]])
        arrivals[m] = begin(m)
    pub_a = publish_gather(0, pub_a)
    arrivals[1] = slice_z(1, arrivals[1])
    pub_b = publish_z(1, pub_b)
    qacc[3] = product(0, local[3], cnt[0, 0, local[3]])
    arrivals[3] = begin(3)
    for m in (2, 3):
        arrivals[m] = slice_z(m, arrivals[m])
    pub_a = publish_last(0, pub_a)
    merge1 = flood(1, rows_of(1, arrivals[1]))
    pub_b = publish_gather(1, pub_b)
    last2 = fold_on(live[0], folds[0], relayed2)
    for m in (2, 3):
        rows = rows_of(m, arrivals[m])
        ys, yr = slices[m][4:]
        for k in range(ny):
            ys[k] = rows[:, k * low : (k + 1) * low]
        arrivals[m] = scatter_y(ys, yr)
    solved1, spread1 = solve(1, merge1)
    pub_a.wait()
    arrivals[2].wait()
    piece = total(slices[2][4][y], slices[2][5])
    merge2 = flood(2, piece - jnp.dot(solved1, coupling(1, 2), preferred_element_type=F32))
    bulk(0)
    pub_b = publish_last(1, pub_b)
    sum_tiles(3, (direct3, last3))
    arrivals[3].wait()
    piece = total(slices[3][4][y], slices[3][5])
    pub_b.wait()
    piece = piece - jnp.dot(solved1, coupling(1, 3), preferred_element_type=F32)
    solved2, spread2 = solve(2, merge2)
    merge3 = flood(3, piece - jnp.dot(solved2, coupling(2, 3), preferred_element_type=F32))
    keep(1, share(1, spread1))
    bulk(1)
    for tile in range(tiles):
        upd[tile] = held[tile].astype(BF16)
    relayed, direct = fold(upd, folds[2])
    _, spread3 = solve(3, merge3)
    shared = share(2, spread2)
    sum_tiles(2, (direct2, last2))
    last = fold_on(upd, folds[2], relayed)
    keep(2, shared)
    direct.wait()
    last.wait()
    half = rhs // 2
    for i in range(2):
        acc[i] = folded(held[x], folds[2], i)
    for i in range(2):
        acc[i] = take(2, i)
    fin, got = folds[3]
    up, down = device(after(1), y, z, c), device(after(n_leaf - 1), y, z, c)
    shared = share(3, spread3)
    sent = []
    for i in (c, 1 - c):
        fin[i] = take(3, i).astype(BF16)
        sent.append(exchange([(fin.at[i], got.at[0, i], up), (fin.at[i], got.at[1, i], down)], got.at[0]))
        drains.append(fetch(fin.at[i], upd_o.at[x, pl.ds(pl.multiple_of(i * half, half), half)]))
        if len(sent) == 1:
            keep(3, shared)
    passed = []
    for i, k, there in ((c, 0, up), (1 - c, 1, down)):
        sent[k].wait()
        passed.append(exchange([(got.at[k, i], got.at[2, i], there)], got.at[2, i]))
    for k, origin in ((0, after(n_leaf - 1)), (1, after(1))):
        for i in range(2):
            drains.append(fetch(got.at[k, i], upd_o.at[origin, pl.ds(i * half, half)]))
    for i, arrival in zip((c, 1 - c), passed):
        arrival.wait()
        drains.append(fetch(got.at[2, i], upd_o.at[after(2), pl.ds(pl.multiple_of(i * half, half), half)]))
    for copy in drains:
        copy.wait()


def settle(solved_h, updated_h, solved_o, updated_o, a, b, sem):
    ways = []
    for i, (src, mid, dst) in enumerate(((solved_h, a, solved_o), (updated_h, b, updated_o))):
        for k in range(src.shape[0]):
            spot = 2 * (i * src.shape[0] + k)
            ways.append(
                (
                    pltpu.make_async_copy(src.at[k], mid.at[k], sem.at[spot]),
                    pltpu.make_async_copy(mid.at[k], dst.at[k], sem.at[spot + 1]),
                )
            )
    for into, _ in ways:
        into.start()
    for into, out in ways:
        into.wait()
        out.start()
    for _, out in ways:
        out.wait()


def on_device(grid, n_leaf, right_side, panels, tile_counts, diag_leaf, diag_pair, diag_root, sup_rows):
    ny, nz, nc = grid
    levels, _, tiles, wide, _ = panels.shape
    rhs = right_side.shape[2]
    mid, part, low = rhs // nc, rhs // nc // nz, wide // ny
    step = wide // nc // nz
    slices, floods = [], []
    for m in range(levels):
        slices.append(
            [
                pltpu.VMEM((nc, mid, wide), BF16),
                pltpu.VMEM((mid, wide), BF16),
                pltpu.VMEM((nz, part, wide), BF16),
                pltpu.VMEM((nz - 1, part, wide), BF16),
            ]
        )
        if m > 1:
            slices[m] += [pltpu.VMEM((ny, part, low), BF16), pltpu.VMEM((ny - 1, part, low), BF16)]
        piece, kind = ((part, wide), BF16) if m < 2 else ((part, low), F32)
        floods.append([pltpu.VMEM(piece, kind), pltpu.VMEM((meeting(m, n_leaf) * ny, *piece), kind)])
    pub = [
        [
            pltpu.VMEM((nc, pairs, wide // nc, wide), BF16),
            pltpu.VMEM((pairs, wide // nc, wide), BF16),
            pltpu.VMEM((ny, pairs, wide // nc, low), BF16),
            pltpu.VMEM((ny - 1, pairs, wide // nc, low), BF16),
            pltpu.VMEM((nz, pairs, step, low), BF16),
            pltpu.VMEM((nz - 1, pairs, step, low), BF16),
            pltpu.VMEM((nc, nz, pairs, step, low), BF16),
        ]
        for pairs in map(len, BATCHES)
    ]
    scratch = [
        pltpu.VMEM((tiles, rhs, wide), BF16),
        [pltpu.VMEM((tiles, wide, wide), BF16)] * levels,
        pltpu.VMEM((1, wide, wide), BF16),
        pltpu.VMEM((2, wide, wide), BF16),
        pltpu.VMEM((2, wide, wide), BF16),
        pltpu.VMEM((tiles, rhs, wide), F32),
        pltpu.VMEM((levels, rhs, wide), F32),
        pltpu.VMEM((levels, nc, nz, part, wide), BF16),
        [pltpu.VMEM((tiles, wide, wide), BF16)] * 2,
        pltpu.VMEM((2, wide, wide), BF16),
        pltpu.VMEM((2, mid, wide), F32),
        pltpu.VMEM((tiles, rhs, wide), BF16),
        [[pltpu.VMEM((2, length // 2, wide), BF16)] * 4 for length in (wide, wide, rhs)]
        + [[pltpu.VMEM((2, rhs // 2, wide), BF16), pltpu.VMEM((n_leaf - 1, 2, rhs // 2, wide), BF16)]],
        slices,
        floods,
        pub,
        pltpu.SemaphoreType.DMA((SEMS,)),
    ]
    anywhere, scalars = pl.BlockSpec(memory_space=pl.ANY), pl.BlockSpec(memory_space=pltpu.SMEM)
    solved, updated = pl.pallas_call(
        functools.partial(kernel, grid, n_leaf),
        out_shape=(
            jax.ShapeDtypeStruct((levels, nc, nz, part, wide), BF16),
            jax.ShapeDtypeStruct((tiles, rhs, wide), BF16),
        ),
        in_specs=[scalars, scalars] + [anywhere] * 5,
        out_specs=(anywhere, anywhere),
        scratch_shapes=scratch,
        compiler_params=pltpu.CompilerParams(
            collective_id=0, has_side_effects=True, vmem_limit_bytes=56 * 2**20
        ),
    )(sup_rows, tile_counts, right_side, panels, diag_leaf, diag_pair, diag_root)
    shapes = [solved.shape, updated.shape]
    solved, updated = pl.pallas_call(
        settle,
        out_shape=tuple(jax.ShapeDtypeStruct(shape, BF16) for shape in shapes),
        in_specs=[anywhere] * 2,
        out_specs=(anywhere, anywhere),
        scratch_shapes=[pltpu.VMEM(shape, BF16) for shape in shapes]
        + [pltpu.SemaphoreType.DMA((2 * (levels + tiles),))],
        compiler_params=pltpu.CompilerParams(vmem_limit_bytes=56 * 2**20),
    )(solved, updated)
    return solved.reshape(levels, 1, rhs, wide), updated


def solution(mesh):
    placed = (
        P("leaf", "row", None, None),
        P(None, "leaf", "row", None, None),
        P(None, "leaf", "row"),
        P("leaf", None, None),
        P(),
        P(),
        P(),
    )
    return jax.shard_map(
        functools.partial(on_device, GRIDS[mesh.shape["row"]], mesh.shape["leaf"]),
        mesh=mesh,
        in_specs=placed,
        out_specs=(P(None, "leaf", None, None), P("row", None, None)),
        check_vma=False,
    )
```

```python
import functools

import jax
import jax.numpy as jnp
from jax import lax
from jax.experimental import pallas as pl
from jax.experimental.pallas import tpu as pltpu
from jax.sharding import PartitionSpec as P

MESH = pl.DeviceIdType.MESH
F32, BF16 = jnp.float32, jnp.bfloat16
BATCHES = (((1, 2),), ((1, 3), (2, 3)))
GRIDS = {64: (4, 8, 2), 8: (2, 2, 2)}
SEMS = 128


def meeting(level, n_leaf):
    return (1, 2, n_leaf, n_leaf)[level]


def kernel(grid, n_leaf, sup, cnt, rs_h, pan_h, dl_h, dp_h, dr_h, sol_o, upd_o, *scratch):
    ny, nz, nc = grid
    (rs, pan, dl, dp, dr, held, qacc, sol, live, sums, acc, upd, folds, slices, floods, pub, sem) = scratch
    levels, (tiles, wide, _) = len(pan), pan[0].shape
    rhs = rs.shape[1]
    low, mid, part = wide // ny, rhs // nc, rhs // nc // nz
    x, r = lax.axis_index("leaf"), lax.axis_index("row")
    y, z, c = r // (nz * nc), (r // nc) % nz, r % nc
    used = [0]
    drains = []

    def device(x_, y_, z_, c_):
        return (x_, (y_ * nz + z_) * nc + c_)

    def fresh():
        used[0] += 1
        assert used[0] <= SEMS
        return sem.at[used[0] - 1]

    def fetch(src, dst):
        copy = pltpu.make_async_copy(src, dst, fresh())
        copy.start()
        return copy

    def exchange(copies, whole):
        out, got = fresh(), fresh()
        for src, dst, dev in copies:
            pltpu.make_async_remote_copy(
                src_ref=src, dst_ref=dst, send_sem=out, recv_sem=got, device_id=dev, device_id_type=MESH
            ).start()
        drains.append(pltpu.make_async_copy(whole, whole, out))
        return pltpu.make_async_copy(whole, whole, got)

    def to_core(src, dst):
        return exchange([(src, dst, device(x, y, z, 1 - c))], dst)

    def scatter_z(src, dst):
        return exchange([(src.at[(z + k) % nz], dst.at[k - 1], device(x, y, (z + k) % nz, c)) for k in range(1, nz)], dst)

    def scatter_y(src, dst):
        return exchange([(src.at[(y + k) % ny], dst.at[k - 1], device(x, (y + k) % ny, z, c)) for k in range(1, ny)], dst)

    def gather_z(ref):
        return exchange(
            [(ref.at[z], ref.at[z], device(x, y, (z + k) % nz, c)) for k in range(1, nz)], ref.at[pl.ds(0, nz - 1)]
        )

    def total(mine, others):
        value = mine.astype(F32)
        for k in range(others.shape[0]):
            value = value + others[k].astype(F32)
        return value

    barrier = pltpu.get_barrier_semaphore()
    peers = [device(x, y, z, 1 - c)]
    peers += [device(x, y, (z + k) % nz, c) for k in range(1, nz)]
    peers += [device(x ^ i, (y + j) % ny, z, c) for i in range(n_leaf) for j in range(ny) if i or j]
    for dev in peers:
        pl.semaphore_signal(barrier, inc=1, device_id=dev, device_id_type=MESH)

    ready = {"rs": fetch(rs_h.at[0], rs), "d0": fetch(dl_h, dl)}
    for level, name in ((1, "p1"), (2, "p2"), (3, "p3"), (0, "p0")):
        ready[name] = fetch(pan_h.at[level, 0], pan[level])
    ready["d1"] = fetch(dp_h, dp)
    ready["d2"] = fetch(dr_h, dr)
    waited = set()

    def need(name):
        if name not in waited:
            waited.add(name)
            ready[name].wait()

    owner = [jnp.where(lax.div(sup[m], tiles) == r, 1.0, 0.0).astype(F32) for m in range(levels)]
    local = [lax.rem(sup[m], tiles) for m in range(levels)]
    columns = lax.broadcasted_iota(jnp.int32, (1, wide), 1)

    def product(level, tile, count):
        done = sol[level].reshape(rhs, wide)
        term = jnp.dot(done, pan[level][tile], preferred_element_type=F32)
        return jnp.where(columns < count, term, 0.0)

    def update(level, tile):
        count = cnt[level, 0, tile]
        for m in range(level + 1):
            count = jnp.where(sup[m] == r * tiles + tile, 0, count)
        term = product(level, tile, count)
        before = rs[tile].astype(F32) if level == 0 else held[tile]
        held[tile] = before - term

    def bulk(level):
        need(f"p{level}")

        def one(tile, carry):
            update(level, tile)
            return carry

        lax.fori_loop(0, tiles, one, 0)

    def prepare(m):
        qs = slices[m][0]
        rows = rs[local[m]].astype(F32)
        if m:
            rows = rows - qacc[m]
        rows = (rows * owner[m]).astype(BF16)
        for half in range(nc):
            qs[half] = rows[half * mid : (half + 1) * mid]

    def begin(m):
        qs, qr = slices[m][:2]
        return to_core(qs.at[1 - c], qr)

    def columns_y(m, arrival):
        qs, qr, ys, yr = slices[m][:4]
        arrival.wait()
        both = (qs[c].astype(F32) + qr[...].astype(F32)).astype(BF16)
        for k in range(ny):
            ys[k] = both[:, k * low : (k + 1) * low]
        return scatter_y(ys, yr)

    def rows_z(m, arrival):
        ys, yr, zs, zr = slices[m][2:]
        arrival.wait()
        zs[...] = total(ys[y], yr).astype(BF16).reshape(nz, part, low)
        return scatter_z(zs, zr)

    def piece_of(m, arrival):
        zs, zr = slices[m][4:]
        arrival.wait()
        return total(zs[z], zr)

    def slice_z(m, arrival):
        qs, qr, zs, zr = slices[m][:4]
        arrival.wait()
        both = qs[c].astype(F32) + qr[...].astype(F32)
        zs[...] = both.astype(BF16).reshape(nz, part, wide)
        return scatter_z(zs, zr)

    def rows_of(m, arrival):
        zs, zr = slices[m][2:4]
        arrival.wait()
        return total(zs[z], zr).astype(BF16)

    def flood(m, value):
        n = meeting(m, n_leaf)
        cs, cr = floods[m]
        own = (x % n) * ny + y
        cs[...] = value
        cr[own] = value
        return exchange(
            [(cs, cr.at[own], device(x ^ a, (y + b) % ny, z, c)) for a in range(n) for b in range(ny) if a or b],
            cr.at[pl.ds(0, n * ny - 1)],
        )

    def solve(m, arrival):
        n = meeting(m, n_leaf)
        cr = floods[m][1]
        arrival.wait()
        if m < 2:
            merged = cr[0].astype(F32)
            for k in range(1, n * ny):
                merged = merged + cr[k].astype(F32)
            merged = merged.astype(BF16)
        else:
            parts = []
            for k in range(ny):
                value = cr[k]
                for a in range(1, n):
                    value = value + cr[a * ny + k]
                parts.append(value.astype(BF16))
            merged = jnp.concatenate(parts, axis=1)
        need(("d0", "d1", "d2", "d2")[m])
        inverse = dl[0] if m == 0 else dp[x // 2] if m == 1 else dr[m - 2]
        solved = jnp.dot(merged, inverse, preferred_element_type=F32).astype(BF16)
        sol[m, c, z] = solved
        return solved, gather_z(sol.at[m, c])

    def share(m, arrival):
        arrival.wait()
        return to_core(sol.at[m, c], sol.at[m, c])

    def keep(m, arrival):
        arrival.wait()
        drains.append(fetch(sol.at[m], sol_o.at[m]))

    def publish_prepare(batch):
        pc = pub[batch][0]
        for i, (level, m) in enumerate(BATCHES[batch]):
            need(f"p{level}")
            alive = jnp.where(columns < cnt[level, 0, local[m]], owner[m], 0.0).astype(BF16)
            tile = pan[level][local[m]] * alive
            for half in range(nc):
                pc[half, i] = tile[half * (wide // nc) : (half + 1) * (wide // nc)]

    def publish_core(batch):
        pc, pcr = pub[batch][:2]
        return to_core(pc.at[1 - c], pcr)

    def publish_y(batch, arrival):
        pc, pcr, py, pyr = pub[batch][:4]
        arrival.wait()
        for i in range(len(BATCHES[batch])):
            both = (pc[c, i].astype(F32) + pcr[i].astype(F32)).astype(BF16)
            for k in range(ny):
                py[k, i] = both[:, k * low : (k + 1) * low]
        return scatter_y(py, pyr)

    def publish_z(batch, arrival):
        py, pyr, pz, pzr = pub[batch][2:6]
        arrival.wait()
        step = wide // nc // nz
        for i in range(len(BATCHES[batch])):
            value = py[y, i].astype(F32)
            for k in range(ny - 1):
                value = value + pyr[k, i].astype(F32)
            value = value.astype(BF16)
            for k in range(nz):
                pz[k, i] = value[k * step : (k + 1) * step]
        return scatter_z(pz, pzr)

    def publish_gather(batch, arrival):
        pz, pzr, pf = pub[batch][4:]
        arrival.wait()
        pf[c, z] = total(pz[z], pzr).astype(BF16)
        return gather_z(pf.at[c])

    def publish_last(batch, arrival):
        pf = pub[batch][6]
        arrival.wait()
        return to_core(pf.at[c], pf.at[c])

    def coupling(level, m):
        batch = 0 if (level, m) in BATCHES[0] else 1
        return pub[batch][6][:, :, BATCHES[batch].index((level, m))].reshape(wide, low)

    def after(k):
        return (x + k) % n_leaf

    up, down = device(after(1), y, z, c), device(after(n_leaf - 1), y, z, c)

    def fold_far(src, bufs):
        relay = bufs[0]
        half = relay.shape[1]
        far, first, second = after(2), pl.ds(0, half), pl.ds(half, half)
        return exchange([(src.at[far, first], relay.at[0], up), (src.at[far, second], relay.at[1], down)], relay)

    def fold_near(src, bufs, piece=0, pieces=1):
        near = bufs[1]
        half, size = near.shape[1], near.shape[1] // pieces
        rows, first, second = pl.ds(piece * size, size), pl.ds(piece * size, size), pl.ds(half + piece * size, size)
        return exchange(
            [
                (src.at[after(1), second], near.at[1, rows], up),
                (src.at[after(n_leaf - 1), first], near.at[0, rows], down),
            ],
            near.at[:, rows],
        )

    def fold_on(src, bufs, piece=0, pieces=1):
        relay, _, out, last = bufs
        half, size = relay.shape[1], relay.shape[1] // pieces
        a, b = piece * size, (piece + 1) * size
        out[0, a:b] = (src[after(1), a:b].astype(F32) + relay[0, a:b].astype(F32)).astype(BF16)
        out[1, a:b] = (src[after(n_leaf - 1), half + a : half + b].astype(F32) + relay[1, a:b].astype(F32)).astype(BF16)
        rows = pl.ds(a, size)
        return exchange([(out.at[0, rows], last.at[0, rows], up), (out.at[1, rows], last.at[1, rows], down)], last.at[:, rows])

    def folded(mine, bufs, i):
        _, near, _, last = bufs
        half = near.shape[1]
        return mine[i * half : (i + 1) * half].astype(F32) + near[i].astype(F32) + last[i].astype(F32)

    def mask_tiles(level):
        need(f"p{level}")
        into = live[level - 2]

        def one(tile, carry):
            count = cnt[level, 0, tile]
            for m in range(level + 1):
                count = jnp.where(sup[m] == r * tiles + tile, 0, count)
            into[tile] = pan[level][tile] * jnp.where(columns < count, 1.0, 0.0).astype(BF16)
            return carry

        lax.fori_loop(0, tiles, one, 0)

    def sum_tiles(level, arrivals):
        for arrival in arrivals:
            arrival.wait()
        half = wide // 2
        for i in range(2):
            sums[level - 2, i * half : (i + 1) * half] = folded(live[level - 2][x], folds[level - 2], i).astype(BF16)

    def take(level, half):
        done = sol[level, half].reshape(mid, wide)
        return acc[half] - jnp.dot(done, sums[level - 2], preferred_element_type=F32)

    need("rs")
    prepare(0)
    pl.semaphore_wait(barrier, len(peers))
    arrival = begin(0)
    publish_prepare(0)
    pub_a = publish_core(0)
    arrival = slice_z(0, arrival)
    publish_prepare(1)
    pub_b = publish_core(1)
    mask_tiles(3)
    relayed3 = fold_far(live[1], folds[1])
    direct3 = fold_near(live[1], folds[1])
    arrival = flood(0, rows_of(0, arrival))
    pub_a = publish_y(0, pub_a)
    pub_b = publish_y(1, pub_b)
    mask_tiles(2)
    _, arrival = solve(0, arrival)
    pub_a = publish_z(0, pub_a)
    relayed3.wait()
    last3 = fold_on(live[1], folds[1])
    relayed2 = fold_far(live[0], folds[0])
    direct2 = [fold_near(live[0], folds[0], 0, 2)]
    keep(0, share(0, arrival))
    need("p0")
    arrivals = {}

    def depart(m):
        qacc[m] = product(0, local[m], cnt[0, 0, local[m]])
        prepare(m)
        arrivals[m] = begin(m)

    depart(1)
    depart(2)
    arrivals[1] = slice_z(1, arrivals[1])
    pub_a = publish_gather(0, pub_a)
    arrivals[2] = columns_y(2, arrivals[2])
    depart(3)
    pub_b = publish_z(1, pub_b)
    arrivals[3] = columns_y(3, arrivals[3])
    merge1 = flood(1, rows_of(1, arrivals[1]))
    for m in (2, 3):
        arrivals[m] = rows_z(m, arrivals[m])
    direct2.append(fold_near(live[0], folds[0], 1, 2))
    relayed2.wait()
    last2 = [fold_on(live[0], folds[0], 0, 2)]
    pub_a = publish_last(0, pub_a)
    pub_b = publish_gather(1, pub_b)
    solved1, spread1 = solve(1, merge1)
    pub_a.wait()
    piece = piece_of(2, arrivals[2])
    merge2 = flood(2, piece - jnp.dot(solved1, coupling(1, 2), preferred_element_type=F32))
    last2.append(fold_on(live[0], folds[0], 1, 2))
    pub_b = publish_last(1, pub_b)
    bulk(0)
    sum_tiles(3, (direct3, last3))
    piece = piece_of(3, arrivals[3])
    pub_b.wait()
    piece = piece - jnp.dot(solved1, coupling(1, 3), preferred_element_type=F32)
    solved2, spread2 = solve(2, merge2)
    merge3 = flood(3, piece - jnp.dot(solved2, coupling(2, 3), preferred_element_type=F32))
    keep(1, share(1, spread1))
    need("p1")

    def settle_base(tile):
        update(1, tile)
        upd[tile] = held[tile].astype(BF16)

    settle_base(after(2))
    relayed = fold_far(upd, folds[2])
    settle_base(after(1))
    settle_base(after(n_leaf - 1))
    direct = fold_near(upd, folds[2])
    update(1, x)
    _, spread3 = solve(3, merge3)
    relayed.wait()
    last = fold_on(upd, folds[2])
    shared = share(2, spread2)
    sum_tiles(2, direct2 + last2)
    keep(2, shared)
    direct.wait()
    last.wait()
    half = rhs // 2
    for i in range(2):
        acc[i] = folded(held[x], folds[2], i)
    for i in range(2):
        acc[i] = take(2, i)
    fin, got = folds[3]
    shared = share(3, spread3)
    sent = []
    for i in (c, 1 - c):
        fin[i] = take(3, i).astype(BF16)
        sent.append(exchange([(fin.at[i], got.at[0, i], up), (fin.at[i], got.at[1, i], down)], got.at[0]))
        drains.append(fetch(fin.at[i], upd_o.at[x, pl.ds(pl.multiple_of(i * half, half), half)]))
        if len(sent) == 1:
            keep(3, shared)
    passed = []
    for i, k, there in ((c, 0, up), (1 - c, 1, down)):
        sent[k].wait()
        passed.append(exchange([(got.at[k, i], got.at[2, i], there)], got.at[2, i]))
    for k, origin in ((0, after(n_leaf - 1)), (1, after(1))):
        for i in range(2):
            drains.append(fetch(got.at[k, i], upd_o.at[origin, pl.ds(i * half, half)]))
    for i, arrival in zip((c, 1 - c), passed):
        arrival.wait()
        drains.append(fetch(got.at[2, i], upd_o.at[after(2), pl.ds(pl.multiple_of(i * half, half), half)]))
    for copy in drains:
        copy.wait()


def settle(solved_h, updated_h, solved_o, updated_o, a, b, sem):
    ways = []
    for i, (src, mid, dst) in enumerate(((solved_h, a, solved_o), (updated_h, b, updated_o))):
        for k in range(src.shape[0]):
            spot = 2 * (i * src.shape[0] + k)
            ways.append(
                (
                    pltpu.make_async_copy(src.at[k], mid.at[k], sem.at[spot]),
                    pltpu.make_async_copy(mid.at[k], dst.at[k], sem.at[spot + 1]),
                )
            )
    for into, _ in ways:
        into.start()
    for into, out in ways:
        into.wait()
        out.start()
    for _, out in ways:
        out.wait()


def on_device(grid, n_leaf, right_side, panels, tile_counts, diag_leaf, diag_pair, diag_root, sup_rows):
    ny, nz, nc = grid
    levels, _, tiles, wide, _ = panels.shape
    rhs = right_side.shape[2]
    mid, part, low = rhs // nc, rhs // nc // nz, wide // ny
    step = wide // nc // nz
    slices, floods = [], []
    for m in range(levels):
        spread = [((nz, part), wide)] if m < 2 else [((ny, mid), low), ((nz, part), low)]
        slices.append([pltpu.VMEM((nc, mid, wide), BF16), pltpu.VMEM((mid, wide), BF16)])
        for (ways, rows), length in spread:
            slices[m] += [pltpu.VMEM((ways, rows, length), BF16), pltpu.VMEM((ways - 1, rows, length), BF16)]
        piece, kind = ((part, wide), BF16) if m < 2 else ((part, low), F32)
        floods.append([pltpu.VMEM(piece, kind), pltpu.VMEM((meeting(m, n_leaf) * ny, *piece), kind)])
    pub = [
        [
            pltpu.VMEM((nc, pairs, wide // nc, wide), BF16),
            pltpu.VMEM((pairs, wide // nc, wide), BF16),
            pltpu.VMEM((ny, pairs, wide // nc, low), BF16),
            pltpu.VMEM((ny - 1, pairs, wide // nc, low), BF16),
            pltpu.VMEM((nz, pairs, step, low), BF16),
            pltpu.VMEM((nz - 1, pairs, step, low), BF16),
            pltpu.VMEM((nc, nz, pairs, step, low), BF16),
        ]
        for pairs in map(len, BATCHES)
    ]
    scratch = [
        pltpu.VMEM((tiles, rhs, wide), BF16),
        [pltpu.VMEM((tiles, wide, wide), BF16)] * levels,
        pltpu.VMEM((1, wide, wide), BF16),
        pltpu.VMEM((2, wide, wide), BF16),
        pltpu.VMEM((2, wide, wide), BF16),
        pltpu.VMEM((tiles, rhs, wide), F32),
        pltpu.VMEM((levels, rhs, wide), F32),
        pltpu.VMEM((levels, nc, nz, part, wide), BF16),
        [pltpu.VMEM((tiles, wide, wide), BF16)] * 2,
        pltpu.VMEM((2, wide, wide), BF16),
        pltpu.VMEM((2, mid, wide), F32),
        pltpu.VMEM((tiles, rhs, wide), BF16),
        [[pltpu.VMEM((2, length // 2, wide), BF16)] * 4 for length in (wide, wide, rhs)]
        + [[pltpu.VMEM((2, rhs // 2, wide), BF16), pltpu.VMEM((n_leaf - 1, 2, rhs // 2, wide), BF16)]],
        slices,
        floods,
        pub,
        pltpu.SemaphoreType.DMA((SEMS,)),
    ]
    anywhere, scalars = pl.BlockSpec(memory_space=pl.ANY), pl.BlockSpec(memory_space=pltpu.SMEM)
    solved, updated = pl.pallas_call(
        functools.partial(kernel, grid, n_leaf),
        out_shape=(
            jax.ShapeDtypeStruct((levels, nc, nz, part, wide), BF16),
            jax.ShapeDtypeStruct((tiles, rhs, wide), BF16),
        ),
        in_specs=[scalars, scalars] + [anywhere] * 5,
        out_specs=(anywhere, anywhere),
        scratch_shapes=scratch,
        compiler_params=pltpu.CompilerParams(
            collective_id=0, has_side_effects=True, vmem_limit_bytes=56 * 2**20
        ),
    )(sup_rows, tile_counts, right_side, panels, diag_leaf, diag_pair, diag_root)
    shapes = [solved.shape, updated.shape]
    solved, updated = pl.pallas_call(
        settle,
        out_shape=tuple(jax.ShapeDtypeStruct(shape, BF16) for shape in shapes),
        in_specs=[anywhere] * 2,
        out_specs=(anywhere, anywhere),
        scratch_shapes=[pltpu.VMEM(shape, BF16) for shape in shapes]
        + [pltpu.SemaphoreType.DMA((2 * (levels + tiles),))],
        compiler_params=pltpu.CompilerParams(vmem_limit_bytes=56 * 2**20),
    )(solved, updated)
    return solved.reshape(levels, 1, rhs, wide), updated


def solution(mesh):
    placed = (
        P("leaf", "row", None, None),
        P(None, "leaf", "row", None, None),
        P(None, "leaf", "row"),
        P("leaf", None, None),
        P(),
        P(),
        P(),
    )
    return jax.shard_map(
        functools.partial(on_device, GRIDS[mesh.shape["row"]], mesh.shape["leaf"]),
        mesh=mesh,
        in_specs=placed,
        out_specs=(P(None, "leaf", None, None), P("row", None, None)),
        check_vma=False,
    )
```

```python
import functools

import jax
import jax.numpy as jnp
from jax import lax
from jax.experimental import pallas as pl
from jax.experimental.pallas import tpu as pltpu
from jax.sharding import PartitionSpec as P

MESH = pl.DeviceIdType.MESH
F32, BF16 = jnp.float32, jnp.bfloat16
BATCHES = (((1, 2),), ((1, 3), (2, 3)))
GRIDS = {64: (4, 8, 2), 8: (2, 2, 2)}
SEMS = 128


def meeting(level, n_leaf):
    return (1, 2, n_leaf, n_leaf)[level]


def kernel(grid, n_leaf, sup, cnt, rs_h, pan_h, dl_h, dp_h, dr_h, sol_o, upd_o, *scratch):
    ny, nz, nc = grid
    (rs, pan, dl, dp, dr, held, first, sol, live, sums, acc, upd, folds, slices, floods, pub, sem) = scratch
    levels, (tiles, wide, _) = len(pan), pan[0].shape
    rhs = rs.shape[1]
    low, mid, part = wide // ny, rhs // nc, rhs // nc // nz
    x, r = lax.axis_index("leaf"), lax.axis_index("row")
    y, z, c = r // (nz * nc), (r // nc) % nz, r % nc
    used = [0]
    drains = []

    def device(x_, y_, z_, c_):
        return (x_, (y_ * nz + z_) * nc + c_)

    def fresh():
        used[0] += 1
        assert used[0] <= SEMS
        return sem.at[used[0] - 1]

    def fetch(src, dst):
        copy = pltpu.make_async_copy(src, dst, fresh())
        copy.start()
        return copy

    def exchange(copies, whole):
        out, got = fresh(), fresh()
        for src, dst, dev in copies:
            pltpu.make_async_remote_copy(
                src_ref=src, dst_ref=dst, send_sem=out, recv_sem=got, device_id=dev, device_id_type=MESH
            ).start()
        drains.append(pltpu.make_async_copy(whole, whole, out))
        return pltpu.make_async_copy(whole, whole, got)

    def to_core(src, dst):
        return exchange([(src, dst, device(x, y, z, 1 - c))], dst)

    def scatter_z(src, dst):
        return exchange([(src.at[(z + k) % nz], dst.at[k - 1], device(x, y, (z + k) % nz, c)) for k in range(1, nz)], dst)

    def scatter_y(src, dst):
        return exchange([(src.at[(y + k) % ny], dst.at[k - 1], device(x, (y + k) % ny, z, c)) for k in range(1, ny)], dst)

    def gather_z(ref):
        return exchange(
            [(ref.at[z], ref.at[z], device(x, y, (z + k) % nz, c)) for k in range(1, nz)], ref.at[pl.ds(0, nz - 1)]
        )

    def total(mine, others):
        value = mine.astype(F32)
        for k in range(others.shape[0]):
            value = value + others[k].astype(F32)
        return value

    ready = {"rs": fetch(rs_h.at[0], rs)}
    barrier = pltpu.get_barrier_semaphore()
    peers = [device(x, y, (z + k) % nz, c) for k in sorted(range(1, nz), key=lambda k: abs(k - nz // 2))]
    peers += [device(x ^ i, (y + j) % ny, z, c) for i in range(n_leaf) for j in range(ny) if i or j]
    peers += [device(x, y, z, 1 - c)]
    for dev in peers:
        pl.semaphore_signal(barrier, inc=1, device_id=dev, device_id_type=MESH)

    ready["d0"] = fetch(dl_h, dl)
    for level, name in ((1, "p1"), (2, "p2"), (3, "p3"), (0, "p0")):
        ready[name] = fetch(pan_h.at[level, 0], pan[level])
    ready["d1"] = fetch(dp_h, dp)
    ready["d2"] = fetch(dr_h, dr)
    waited = set()

    def need(name):
        if name not in waited:
            waited.add(name)
            ready[name].wait()

    owner = [jnp.where(lax.div(sup[m], tiles) == r, 1.0, 0.0).astype(F32) for m in range(levels)]
    local = [lax.rem(sup[m], tiles) for m in range(levels)]
    columns = lax.broadcasted_iota(jnp.int32, (1, wide), 1)

    def product(level, tile, count):
        done = sol[level].reshape(rhs, wide)
        term = jnp.dot(done, pan[level][tile], preferred_element_type=F32)
        return jnp.where(columns < count, term, 0.0)

    def update(level, tile):
        count = cnt[level, 0, tile]
        for m in range(level + 1):
            count = jnp.where(sup[m] == r * tiles + tile, 0, count)
        term = product(level, tile, count)
        before = rs[tile].astype(F32) if level == 0 else held[tile]
        held[tile] = before - term

    def bulk(level):
        need(f"p{level}")

        def one(tile, carry):
            update(level, tile)
            return carry

        lax.fori_loop(0, tiles, one, 0)

    def prepare(m):
        qs = slices[m][0]
        rows = rs[local[m]] * owner[m].astype(BF16)
        for half in range(nc):
            qs[half] = rows[half * mid : (half + 1) * mid]

    def begin(m):
        qs, qr = slices[m][:2]
        return to_core(qs.at[1 - c], qr)

    def columns_y(m, arrival):
        ys, yr = slices[m][2:4]
        both = half_of(m, arrival)
        for k in range(ny):
            ys[k] = both[:, k * low : (k + 1) * low]
        return scatter_y(ys, yr)

    def rows_z(m, arrival):
        ys, yr, zs, zr = slices[m][2:]
        arrival.wait()
        zs[...] = total(ys[y], yr).astype(BF16).reshape(nz, part, low)
        return scatter_z(zs, zr)

    def piece_of(m, arrival):
        zs, zr = slices[m][4:]
        arrival.wait()
        return total(zs[z], zr)

    def half_of(m, arrival):
        qs, qr = slices[m][:2]
        arrival.wait()
        both = qs[c].astype(F32) + qr[...].astype(F32)
        if m:
            both = both - jnp.dot(sol[0, c].reshape(mid, wide), first[1][m - 1], preferred_element_type=F32)
        return both.astype(BF16)

    def slice_z(m, arrival):
        zs, zr = slices[m][2:4]
        zs[...] = half_of(m, arrival).reshape(nz, part, wide)
        return scatter_z(zs, zr)

    def rows_of(m, arrival):
        zs, zr = slices[m][2:4]
        arrival.wait()
        return total(zs[z], zr).astype(BF16)

    def flood(m, value):
        n = meeting(m, n_leaf)
        cs, cr = floods[m]
        own = (x % n) * ny + y
        cs[...] = value
        cr[own] = value
        return exchange(
            [(cs, cr.at[own], device(x ^ a, (y + b) % ny, z, c)) for a in range(n) for b in range(ny) if a or b],
            cr.at[pl.ds(0, n * ny - 1)],
        )

    def solve(m, arrival):
        n = meeting(m, n_leaf)
        cr = floods[m][1]
        arrival.wait()
        if m < 2:
            merged = cr[0].astype(F32)
            for k in range(1, n * ny):
                merged = merged + cr[k].astype(F32)
            merged = merged.astype(BF16)
        else:
            parts = []
            for k in range(ny):
                value = cr[k]
                for a in range(1, n):
                    value = value + cr[a * ny + k]
                parts.append(value.astype(BF16))
            merged = jnp.concatenate(parts, axis=1)
        need(("d0", "d1", "d2", "d2")[m])
        inverse = dl[0] if m == 0 else dp[x // 2] if m == 1 else dr[m - 2]
        solved = jnp.dot(merged, inverse, preferred_element_type=F32).astype(BF16)
        sol[m, c, z] = solved
        return solved, gather_z(sol.at[m, c])

    def share(m, arrival):
        arrival.wait()
        return to_core(sol.at[m, c], sol.at[m, c])

    def keep(m, arrival):
        arrival.wait()
        drains.append(fetch(sol.at[m], sol_o.at[m]))

    def first_core():
        need("p0")
        for m in range(1, levels):
            alive = jnp.where(columns < cnt[0, 0, local[m]], owner[m], 0.0).astype(BF16)
            first[0][m - 1] = pan[0][local[m]] * alive
        return to_core(first[0], first[1])

    def publish_prepare(batch):
        pc = pub[batch][0]
        for i, (level, m) in enumerate(BATCHES[batch]):
            need(f"p{level}")
            alive = jnp.where(columns < cnt[level, 0, local[m]], owner[m], 0.0).astype(BF16)
            tile = pan[level][local[m]] * alive
            for half in range(nc):
                pc[half, i] = tile[half * (wide // nc) : (half + 1) * (wide // nc)]

    def publish_core(batch):
        pc, pcr = pub[batch][:2]
        return to_core(pc.at[1 - c], pcr)

    def publish_y(batch, arrival):
        pc, pcr, py, pyr = pub[batch][:4]
        arrival.wait()
        for i in range(len(BATCHES[batch])):
            both = (pc[c, i].astype(F32) + pcr[i].astype(F32)).astype(BF16)
            for k in range(ny):
                py[k, i] = both[:, k * low : (k + 1) * low]
        return scatter_y(py, pyr)

    def publish_z(batch, arrival):
        py, pyr, pz, pzr = pub[batch][2:6]
        arrival.wait()
        step = wide // nc // nz
        for i in range(len(BATCHES[batch])):
            value = py[y, i].astype(F32)
            for k in range(ny - 1):
                value = value + pyr[k, i].astype(F32)
            value = value.astype(BF16)
            for k in range(nz):
                pz[k, i] = value[k * step : (k + 1) * step]
        return scatter_z(pz, pzr)

    def publish_gather(batch, arrival):
        pz, pzr, pf = pub[batch][4:]
        arrival.wait()
        pf[c, z] = total(pz[z], pzr).astype(BF16)
        return gather_z(pf.at[c])

    def publish_last(batch, arrival):
        pf = pub[batch][6]
        arrival.wait()
        return to_core(pf.at[c], pf.at[c])

    def coupling(level, m):
        batch = 0 if (level, m) in BATCHES[0] else 1
        return pub[batch][6][:, :, BATCHES[batch].index((level, m))].reshape(wide, low)

    def after(k):
        return (x + k) % n_leaf

    up, down = device(after(1), y, z, c), device(after(n_leaf - 1), y, z, c)

    def fold_far(src, bufs, piece=0, pieces=1):
        relay = bufs[0]
        half, size = relay.shape[1], relay.shape[1] // pieces
        far, rows, second = after(2), pl.ds(piece * size, size), pl.ds(half + piece * size, size)
        return exchange(
            [(src.at[far, rows], relay.at[0, rows], up), (src.at[far, second], relay.at[1, rows], down)],
            relay.at[:, rows],
        )

    def fold_near(src, bufs):
        near = bufs[1]
        half = near.shape[1]
        first, second = pl.ds(0, half), pl.ds(half, half)
        return exchange(
            [(src.at[after(1), second], near.at[1], up), (src.at[after(n_leaf - 1), first], near.at[0], down)], near
        )

    def fold_on(src, bufs, piece=0, pieces=1):
        relay, _, out, last = bufs
        half, size = relay.shape[1], relay.shape[1] // pieces
        a, b = piece * size, (piece + 1) * size
        out[0, a:b] = (src[after(1), a:b].astype(F32) + relay[0, a:b].astype(F32)).astype(BF16)
        out[1, a:b] = (src[after(n_leaf - 1), half + a : half + b].astype(F32) + relay[1, a:b].astype(F32)).astype(BF16)
        rows = pl.ds(a, size)
        return exchange([(out.at[0, rows], last.at[0, rows], up), (out.at[1, rows], last.at[1, rows], down)], last.at[:, rows])

    def folded(mine, bufs, i):
        _, near, _, last = bufs
        half = near.shape[1]
        return mine[i * half : (i + 1) * half].astype(F32) + near[i].astype(F32) + last[i].astype(F32)

    def mask_tiles(level):
        need(f"p{level}")
        into = live[level - 2]

        def one(tile, carry):
            count = cnt[level, 0, tile]
            for m in range(level + 1):
                count = jnp.where(sup[m] == r * tiles + tile, 0, count)
            into[tile] = pan[level][tile] * jnp.where(columns < count, 1.0, 0.0).astype(BF16)
            return carry

        lax.fori_loop(0, tiles, one, 0)

    def sum_tiles(level, arrivals):
        for arrival in arrivals:
            arrival.wait()
        half = wide // 2
        for i in range(2):
            sums[level - 2, i * half : (i + 1) * half] = folded(live[level - 2][x], folds[level - 2], i).astype(BF16)

    def take(level, half):
        done = sol[level, half].reshape(mid, wide)
        return acc[half] - jnp.dot(done, sums[level - 2], preferred_element_type=F32)

    need("rs")
    prepare(0)
    pl.semaphore_wait(barrier, len(peers))
    arrival = begin(0)
    publish_prepare(0)
    pub_a = publish_core(0)
    mask_tiles(3)
    relayed3 = fold_far(live[1], folds[1])
    direct3 = fold_near(live[1], folds[1])
    arrival = slice_z(0, arrival)
    publish_prepare(1)
    pub_b = publish_core(1)
    arrivals = {}
    for m in (1, 2, 3):
        prepare(m)
        arrivals[m] = begin(m)
    coupled = first_core()
    arrival = flood(0, rows_of(0, arrival))
    pub_a = publish_y(0, pub_a)
    pub_b = publish_y(1, pub_b)
    mask_tiles(2)
    relayed3.wait()
    last3 = fold_on(live[1], folds[1])
    relayed2 = fold_far(live[0], folds[0])
    _, arrival = solve(0, arrival)
    coupled.wait()
    for m in range(1, levels):
        first[1][m - 1] = first[0][m - 1] + first[1][m - 1]
    pub_a = publish_z(0, pub_a)
    shared0 = share(0, arrival)
    arrivals[1] = slice_z(1, arrivals[1])
    pub_a = publish_gather(0, pub_a)
    arrivals[2] = columns_y(2, arrivals[2])
    pub_b = publish_z(1, pub_b)
    arrivals[3] = columns_y(3, arrivals[3])
    merge1 = flood(1, rows_of(1, arrivals[1]))
    for m in (2, 3):
        arrivals[m] = rows_z(m, arrivals[m])
    direct2 = fold_near(live[0], folds[0])
    pub_a = publish_last(0, pub_a)
    pub_b = publish_gather(1, pub_b)
    solved1, spread1 = solve(1, merge1)
    pub_a.wait()
    piece = piece_of(2, arrivals[2])
    merge2 = flood(2, piece - jnp.dot(solved1, coupling(1, 2), preferred_element_type=F32))
    relayed2.wait()
    last2 = fold_on(live[0], folds[0])
    pub_b = publish_last(1, pub_b)
    keep(0, shared0)
    bulk(0)
    sum_tiles(3, (direct3, last3))
    piece = piece_of(3, arrivals[3])
    pub_b.wait()
    piece = piece - jnp.dot(solved1, coupling(1, 3), preferred_element_type=F32)
    shared1 = share(1, spread1)
    solved2, spread2 = solve(2, merge2)
    merge3 = flood(3, piece - jnp.dot(solved2, coupling(2, 3), preferred_element_type=F32))
    keep(1, shared1)
    need("p1")

    def settle_base(tile):
        update(1, tile)
        upd[tile] = held[tile].astype(BF16)

    settle_base(after(2))
    relayed = [fold_far(upd, folds[2], i, 2) for i in range(2)]
    settle_base(after(1))
    settle_base(after(n_leaf - 1))
    direct = fold_near(upd, folds[2])
    update(1, x)
    _, spread3 = solve(3, merge3)
    last = []
    for i in range(2):
        relayed[i].wait()
        last.append(fold_on(upd, folds[2], i, 2))
    shared = share(2, spread2)
    sum_tiles(2, (direct2, last2))
    keep(2, shared)
    for arrival in (direct, *last):
        arrival.wait()
    half = rhs // 2
    for i in range(2):
        acc[i] = folded(held[x], folds[2], i)
    for i in range(2):
        acc[i] = take(2, i)
    fin, got = folds[3]
    shared = share(3, spread3)
    quarter = half // 2
    early, late = pl.ds(0, quarter), pl.ds(quarter, quarter)

    def send(src, dst, dev):
        return exchange([(src, dst, dev)], src)

    def rows(i):
        return pl.ds(pl.multiple_of(i * half, half), half)

    fin[c] = take(3, c).astype(BF16)
    to_up = send(fin.at[c], got.at[0, c], up)
    others = [send(fin.at[c, early], got.at[1, c, early], down)]
    keep(3, shared)
    fin[1 - c] = take(3, 1 - c).astype(BF16)
    to_down = send(fin.at[1 - c], got.at[1, 1 - c], down)
    others.append(send(fin.at[c, late], got.at[1, c, late], down))
    others.append(send(fin.at[1 - c], got.at[0, 1 - c], up))
    for i in range(2):
        drains.append(fetch(fin.at[i], upd_o.at[x, rows(i)]))
    to_up.wait()
    passed = [send(got.at[0, c], upd_o.at[after(n_leaf - 1), rows(c)], up)]
    to_down.wait()
    passed.append(send(got.at[1, 1 - c], upd_o.at[after(1), rows(1 - c)], down))
    for arrival in others:
        arrival.wait()
    for k, origin in ((0, after(n_leaf - 1)), (1, after(1))):
        for i in range(2):
            drains.append(fetch(got.at[k, i], upd_o.at[origin, rows(i)]))
    for arrival in passed:
        arrival.wait()
    for copy in drains:
        copy.wait()


def settle(solved_h, updated_h, solved_o, updated_o, a, b, sem):
    ways = []
    for i, (src, mid, dst) in enumerate(((solved_h, a, solved_o), (updated_h, b, updated_o))):
        for k in range(src.shape[0]):
            spot = 2 * (i * src.shape[0] + k)
            ways.append(
                (
                    pltpu.make_async_copy(src.at[k], mid.at[k], sem.at[spot]),
                    pltpu.make_async_copy(mid.at[k], dst.at[k], sem.at[spot + 1]),
                )
            )
    for into, _ in ways:
        into.start()
    for into, out in ways:
        into.wait()
        out.start()
    for _, out in ways:
        out.wait()


def on_device(grid, n_leaf, right_side, panels, tile_counts, diag_leaf, diag_pair, diag_root, sup_rows):
    ny, nz, nc = grid
    levels, _, tiles, wide, _ = panels.shape
    rhs = right_side.shape[2]
    mid, part, low = rhs // nc, rhs // nc // nz, wide // ny
    step = wide // nc // nz
    slices, floods = [], []
    for m in range(levels):
        spread = [((nz, part), wide)] if m < 2 else [((ny, mid), low), ((nz, part), low)]
        slices.append([pltpu.VMEM((nc, mid, wide), BF16), pltpu.VMEM((mid, wide), BF16)])
        for (ways, rows), length in spread:
            slices[m] += [pltpu.VMEM((ways, rows, length), BF16), pltpu.VMEM((ways - 1, rows, length), BF16)]
        piece, kind = ((part, wide), BF16) if m < 2 else ((part, low), F32)
        floods.append([pltpu.VMEM(piece, kind), pltpu.VMEM((meeting(m, n_leaf) * ny, *piece), kind)])
    pub = [
        [
            pltpu.VMEM((nc, pairs, wide // nc, wide), BF16),
            pltpu.VMEM((pairs, wide // nc, wide), BF16),
            pltpu.VMEM((ny, pairs, wide // nc, low), BF16),
            pltpu.VMEM((ny - 1, pairs, wide // nc, low), BF16),
            pltpu.VMEM((nz, pairs, step, low), BF16),
            pltpu.VMEM((nz - 1, pairs, step, low), BF16),
            pltpu.VMEM((nc, nz, pairs, step, low), BF16),
        ]
        for pairs in map(len, BATCHES)
    ]
    scratch = [
        pltpu.VMEM((tiles, rhs, wide), BF16),
        [pltpu.VMEM((tiles, wide, wide), BF16)] * levels,
        pltpu.VMEM((1, wide, wide), BF16),
        pltpu.VMEM((2, wide, wide), BF16),
        pltpu.VMEM((2, wide, wide), BF16),
        pltpu.VMEM((tiles, rhs, wide), F32),
        [pltpu.VMEM((levels - 1, wide, wide), BF16)] * 2,
        pltpu.VMEM((levels, nc, nz, part, wide), BF16),
        [pltpu.VMEM((tiles, wide, wide), BF16)] * 2,
        pltpu.VMEM((2, wide, wide), BF16),
        pltpu.VMEM((2, mid, wide), F32),
        pltpu.VMEM((tiles, rhs, wide), BF16),
        [[pltpu.VMEM((2, length // 2, wide), BF16)] * 4 for length in (wide, wide, rhs)]
        + [[pltpu.VMEM((2, rhs // 2, wide), BF16), pltpu.VMEM((2, 2, rhs // 2, wide), BF16)]],
        slices,
        floods,
        pub,
        pltpu.SemaphoreType.DMA((SEMS,)),
    ]
    anywhere, scalars = pl.BlockSpec(memory_space=pl.ANY), pl.BlockSpec(memory_space=pltpu.SMEM)
    solved, updated = pl.pallas_call(
        functools.partial(kernel, grid, n_leaf),
        out_shape=(
            jax.ShapeDtypeStruct((levels, nc, nz, part, wide), BF16),
            jax.ShapeDtypeStruct((tiles, rhs, wide), BF16),
        ),
        in_specs=[scalars, scalars] + [anywhere] * 5,
        out_specs=(anywhere, anywhere),
        scratch_shapes=scratch,
        compiler_params=pltpu.CompilerParams(
            collective_id=0, has_side_effects=True, vmem_limit_bytes=56 * 2**20
        ),
    )(sup_rows, tile_counts, right_side, panels, diag_leaf, diag_pair, diag_root)
    shapes = [solved.shape, updated.shape]
    solved, updated = pl.pallas_call(
        settle,
        out_shape=tuple(jax.ShapeDtypeStruct(shape, BF16) for shape in shapes),
        in_specs=[anywhere] * 2,
        out_specs=(anywhere, anywhere),
        scratch_shapes=[pltpu.VMEM(shape, BF16) for shape in shapes]
        + [pltpu.SemaphoreType.DMA((2 * (levels + tiles),))],
        compiler_params=pltpu.CompilerParams(vmem_limit_bytes=56 * 2**20),
    )(solved, updated)
    return solved.reshape(levels, 1, rhs, wide), updated


def solution(mesh):
    placed = (
        P("leaf", "row", None, None),
        P(None, "leaf", "row", None, None),
        P(None, "leaf", "row"),
        P("leaf", None, None),
        P(),
        P(),
        P(),
    )
    return jax.shard_map(
        functools.partial(on_device, GRIDS[mesh.shape["row"]], mesh.shape["leaf"]),
        mesh=mesh,
        in_specs=placed,
        out_specs=(P(None, "leaf", None, None), P("row", None, None)),
        check_vma=False,
    )
```

```python
import functools

import jax
import jax.numpy as jnp
from jax import lax
from jax.experimental import pallas as pl
from jax.experimental.pallas import tpu as pltpu
from jax.sharding import PartitionSpec as P

MESH = pl.DeviceIdType.MESH
F32, BF16 = jnp.float32, jnp.bfloat16
BATCHES = (((1, 2),), ((1, 3), (2, 3)))
GRIDS = {64: (4, 8, 2), 8: (2, 2, 2)}
SEMS = 128


def meeting(level, n_leaf):
    return (1, 2, n_leaf, n_leaf)[level]


def kernel(grid, n_leaf, sup, cnt, rs_h, pan_h, dl_h, dp_h, dr_h, sol_o, upd_o, *scratch):
    ny, nz, nc = grid
    (rs, pan, dl, dp, dr, held, first, sol, live, sums, acc, upd, folds, slices, floods, pub, sem) = scratch
    levels, (tiles, wide, _) = len(pan), pan[0].shape
    rhs = rs.shape[1]
    low, mid, part = wide // ny, rhs // nc, rhs // nc // nz
    x, r = lax.axis_index("leaf"), lax.axis_index("row")
    y, z, c = r // (nz * nc), (r // nc) % nz, r % nc
    used = [0]
    drains = []

    def device(x_, y_, z_, c_):
        return (x_, (y_ * nz + z_) * nc + c_)

    def fresh():
        used[0] += 1
        assert used[0] <= SEMS
        return sem.at[used[0] - 1]

    def fetch(src, dst):
        copy = pltpu.make_async_copy(src, dst, fresh())
        copy.start()
        return copy

    def exchange(copies, whole):
        out, got = fresh(), fresh()
        for src, dst, dev in copies:
            pltpu.make_async_remote_copy(
                src_ref=src, dst_ref=dst, send_sem=out, recv_sem=got, device_id=dev, device_id_type=MESH
            ).start()
        drains.append(pltpu.make_async_copy(whole, whole, out))
        return pltpu.make_async_copy(whole, whole, got)

    def to_core(src, dst):
        return exchange([(src, dst, device(x, y, z, 1 - c))], dst)

    def scatter_z(src, dst):
        return exchange([(src.at[(z + k) % nz], dst.at[k - 1], device(x, y, (z + k) % nz, c)) for k in range(1, nz)], dst)

    def scatter_y(src, dst):
        return exchange([(src.at[(y + k) % ny], dst.at[k - 1], device(x, (y + k) % ny, z, c)) for k in range(1, ny)], dst)

    def gather_z(ref):
        return exchange(
            [(ref.at[z], ref.at[z], device(x, y, (z + k) % nz, c)) for k in range(1, nz)], ref.at[pl.ds(0, nz - 1)]
        )

    def total(mine, others):
        value = mine.astype(F32)
        for k in range(others.shape[0]):
            value = value + others[k].astype(F32)
        return value

    ready = {"rs": fetch(rs_h.at[0], rs)}
    barrier = pltpu.get_barrier_semaphore()
    peers = [device(x, y, (z + k) % nz, c) for k in sorted(range(1, nz), key=lambda k: abs(k - nz // 2))]
    peers += [device(x ^ i, (y + j) % ny, z, c) for i in range(n_leaf) for j in range(ny) if i or j]
    peers += [device(x, y, z, 1 - c)]
    for dev in peers:
        pl.semaphore_signal(barrier, inc=1, device_id=dev, device_id_type=MESH)

    ready["d0"] = fetch(dl_h, dl)
    for level, name in ((1, "p1"), (2, "p2"), (3, "p3"), (0, "p0")):
        ready[name] = fetch(pan_h.at[level, 0], pan[level])
    ready["d1"] = fetch(dp_h, dp)
    ready["d2"] = fetch(dr_h, dr)
    waited = set()

    def need(name):
        if name not in waited:
            waited.add(name)
            ready[name].wait()

    owner = [jnp.where(lax.div(sup[m], tiles) == r, 1.0, 0.0).astype(F32) for m in range(levels)]
    local = [lax.rem(sup[m], tiles) for m in range(levels)]
    columns = lax.broadcasted_iota(jnp.int32, (1, wide), 1)

    def product(level, tile, count):
        done = sol[level].reshape(rhs, wide)
        term = jnp.dot(done, pan[level][tile], preferred_element_type=F32)
        return jnp.where(columns < count, term, 0.0)

    def update(level, tile):
        count = cnt[level, 0, tile]
        for m in range(level + 1):
            count = jnp.where(sup[m] == r * tiles + tile, 0, count)
        term = product(level, tile, count)
        before = rs[tile].astype(F32) if level == 0 else held[tile]
        held[tile] = before - term

    def bulk(level):
        need(f"p{level}")

        def one(tile, carry):
            update(level, tile)
            return carry

        lax.fori_loop(0, tiles, one, 0)

    def prepare(m):
        qs = slices[m][0]
        rows = rs[local[m]] * owner[m].astype(BF16)
        for half in range(nc):
            qs[half] = rows[half * mid : (half + 1) * mid]

    def begin(m):
        qs, qr = slices[m][:2]
        return to_core(qs.at[1 - c], qr)

    def columns_y(m, arrival):
        ys, yr = slices[m][2:4]
        both = half_of(m, arrival)
        for k in range(ny):
            ys[k] = both[:, k * low : (k + 1) * low]
        return scatter_y(ys, yr)

    def rows_z(m, arrival):
        ys, yr, zs, zr = slices[m][2:]
        arrival.wait()
        zs[...] = total(ys[y], yr).astype(BF16).reshape(nz, part, low)
        return scatter_z(zs, zr)

    def piece_of(m, arrival):
        zs, zr = slices[m][4:]
        arrival.wait()
        return total(zs[z], zr)

    def half_of(m, arrival):
        qs, qr = slices[m][:2]
        arrival.wait()
        both = qs[c].astype(F32) + qr[...].astype(F32)
        if m:
            both = both - jnp.dot(sol[0, c].reshape(mid, wide), first[1][m - 1], preferred_element_type=F32)
        return both.astype(BF16)

    def slice_z(m, arrival):
        zs, zr = slices[m][2:4]
        zs[...] = half_of(m, arrival).reshape(nz, part, wide)
        return scatter_z(zs, zr)

    def rows_of(m, arrival):
        zs, zr = slices[m][2:4]
        arrival.wait()
        return total(zs[z], zr).astype(BF16)

    def flood(m, value):
        n = meeting(m, n_leaf)
        cs, cr = floods[m]
        own = (x % n) * ny + y
        cs[...] = value
        cr[own] = value
        return exchange(
            [(cs, cr.at[own], device(x ^ a, (y + b) % ny, z, c)) for a in range(n) for b in range(ny) if a or b],
            cr.at[pl.ds(0, n * ny - 1)],
        )

    def solve(m, arrival):
        n = meeting(m, n_leaf)
        cr = floods[m][1]
        arrival.wait()
        if m < 2:
            merged = cr[0].astype(F32)
            for k in range(1, n * ny):
                merged = merged + cr[k].astype(F32)
            merged = merged.astype(BF16)
        else:
            parts = []
            for k in range(ny):
                value = cr[k]
                for a in range(1, n):
                    value = value + cr[a * ny + k]
                parts.append(value.astype(BF16))
            merged = jnp.concatenate(parts, axis=1)
        need(("d0", "d1", "d2", "d2")[m])
        inverse = dl[0] if m == 0 else dp[x // 2] if m == 1 else dr[m - 2]
        solved = jnp.dot(merged, inverse, preferred_element_type=F32).astype(BF16)
        sol[m, c, z] = solved
        return solved, gather_z(sol.at[m, c])

    def share(m, arrival):
        arrival.wait()
        return to_core(sol.at[m, c], sol.at[m, c])

    def keep(m, arrival):
        arrival.wait()
        drains.append(fetch(sol.at[m], sol_o.at[m]))

    def first_core():
        need("p0")
        for m in range(1, levels):
            alive = jnp.where(columns < cnt[0, 0, local[m]], owner[m], 0.0).astype(BF16)
            first[0][m - 1] = pan[0][local[m]] * alive
        return to_core(first[0], first[1])

    def publish_prepare(batch):
        pc = pub[batch][0]
        for i, (level, m) in enumerate(BATCHES[batch]):
            need(f"p{level}")
            alive = jnp.where(columns < cnt[level, 0, local[m]], owner[m], 0.0).astype(BF16)
            tile = pan[level][local[m]] * alive
            for half in range(nc):
                pc[half, i] = tile[half * (wide // nc) : (half + 1) * (wide // nc)]

    def publish_core(batch):
        pc, pcr = pub[batch][:2]
        return to_core(pc.at[1 - c], pcr)

    def publish_y(batch, arrival):
        pc, pcr, py, pyr = pub[batch][:4]
        arrival.wait()
        for i in range(len(BATCHES[batch])):
            both = (pc[c, i].astype(F32) + pcr[i].astype(F32)).astype(BF16)
            for k in range(ny):
                py[k, i] = both[:, k * low : (k + 1) * low]
        return scatter_y(py, pyr)

    def publish_z(batch, arrival):
        py, pyr, pz, pzr = pub[batch][2:6]
        arrival.wait()
        step = wide // nc // nz
        for i in range(len(BATCHES[batch])):
            value = py[y, i].astype(F32)
            for k in range(ny - 1):
                value = value + pyr[k, i].astype(F32)
            value = value.astype(BF16)
            for k in range(nz):
                pz[k, i] = value[k * step : (k + 1) * step]
        return scatter_z(pz, pzr)

    def publish_gather(batch, arrival):
        pz, pzr, pf = pub[batch][4:]
        arrival.wait()
        pf[c, z] = total(pz[z], pzr).astype(BF16)
        return gather_z(pf.at[c])

    def publish_last(batch, arrival):
        pf = pub[batch][6]
        arrival.wait()
        return to_core(pf.at[c], pf.at[c])

    def coupling(level, m):
        batch = 0 if (level, m) in BATCHES[0] else 1
        return pub[batch][6][:, :, BATCHES[batch].index((level, m))].reshape(wide, low)

    def after(k):
        return (x + k) % n_leaf

    up, down = device(after(1), y, z, c), device(after(n_leaf - 1), y, z, c)

    def fold_far(src, bufs, piece=0, pieces=1):
        relay = bufs[0]
        half, size = relay.shape[1], relay.shape[1] // pieces
        far, rows, second = after(2), pl.ds(piece * size, size), pl.ds(half + piece * size, size)
        return exchange(
            [(src.at[far, rows], relay.at[0, rows], up), (src.at[far, second], relay.at[1, rows], down)],
            relay.at[:, rows],
        )

    def fold_near(src, bufs):
        near = bufs[1]
        half = near.shape[1]
        first, second = pl.ds(0, half), pl.ds(half, half)
        return exchange(
            [(src.at[after(1), second], near.at[1], up), (src.at[after(n_leaf - 1), first], near.at[0], down)], near
        )

    def fold_on(src, bufs, piece=0, pieces=1):
        relay, _, out, last = bufs
        half, size = relay.shape[1], relay.shape[1] // pieces
        a, b = piece * size, (piece + 1) * size
        out[0, a:b] = (src[after(1), a:b].astype(F32) + relay[0, a:b].astype(F32)).astype(BF16)
        out[1, a:b] = (src[after(n_leaf - 1), half + a : half + b].astype(F32) + relay[1, a:b].astype(F32)).astype(BF16)
        rows = pl.ds(a, size)
        return exchange([(out.at[0, rows], last.at[0, rows], up), (out.at[1, rows], last.at[1, rows], down)], last.at[:, rows])

    def folded(mine, bufs, i):
        _, near, _, last = bufs
        half = near.shape[1]
        return mine[i * half : (i + 1) * half].astype(F32) + near[i].astype(F32) + last[i].astype(F32)

    def mask_tiles(level):
        need(f"p{level}")
        into = live[level - 2]

        def one(tile, carry):
            count = cnt[level, 0, tile]
            for m in range(level + 1):
                count = jnp.where(sup[m] == r * tiles + tile, 0, count)
            into[tile] = pan[level][tile] * jnp.where(columns < count, 1.0, 0.0).astype(BF16)
            return carry

        lax.fori_loop(0, tiles, one, 0)

    def sum_tiles(level, arrivals):
        for arrival in arrivals:
            arrival.wait()
        half = wide // 2
        for i in range(2):
            sums[level - 2, i * half : (i + 1) * half] = folded(live[level - 2][x], folds[level - 2], i).astype(BF16)

    def take(level, half):
        done = sol[level, half].reshape(mid, wide)
        return acc[half] - jnp.dot(done, sums[level - 2], preferred_element_type=F32)

    need("rs")
    prepare(0)
    pl.semaphore_wait(barrier, len(peers))
    arrival = begin(0)
    publish_prepare(0)
    pub_a = publish_core(0)
    mask_tiles(3)
    relayed3 = fold_far(live[1], folds[1])
    direct3 = fold_near(live[1], folds[1])
    arrival = slice_z(0, arrival)
    publish_prepare(1)
    pub_b = publish_core(1)
    arrivals = {}
    for m in (1, 2, 3):
        prepare(m)
        arrivals[m] = begin(m)
    pub_a = publish_y(0, pub_a)
    coupled = first_core()
    arrival = flood(0, rows_of(0, arrival))
    pub_b = publish_y(1, pub_b)
    pub_a = publish_z(0, pub_a)
    mask_tiles(2)
    relayed3.wait()
    last3 = fold_on(live[1], folds[1])
    relayed2 = fold_far(live[0], folds[0])
    _, arrival = solve(0, arrival)
    coupled.wait()
    for m in range(1, levels):
        first[1][m - 1] = first[0][m - 1] + first[1][m - 1]
    pub_a = publish_gather(0, pub_a)
    shared0 = share(0, arrival)
    arrivals[1] = slice_z(1, arrivals[1])
    arrivals[2] = columns_y(2, arrivals[2])
    pub_b = publish_z(1, pub_b)
    arrivals[3] = columns_y(3, arrivals[3])
    pub_a = publish_last(0, pub_a)
    keep(0, shared0)
    bulk(0)
    merge1 = flood(1, rows_of(1, arrivals[1]))
    for m in (2, 3):
        arrivals[m] = rows_z(m, arrivals[m])
    direct2 = fold_near(live[0], folds[0])
    pub_b = publish_gather(1, pub_b)
    solved1, spread1 = solve(1, merge1)
    pub_a.wait()
    piece = piece_of(2, arrivals[2])
    merge2 = flood(2, piece - jnp.dot(solved1, coupling(1, 2), preferred_element_type=F32))
    relayed2.wait()
    last2 = fold_on(live[0], folds[0])
    pub_b = publish_last(1, pub_b)
    piece = piece_of(3, arrivals[3])
    pub_b.wait()
    piece = piece - jnp.dot(solved1, coupling(1, 3), preferred_element_type=F32)
    shared1 = share(1, spread1)
    solved2, spread2 = solve(2, merge2)
    merge3 = flood(3, piece - jnp.dot(solved2, coupling(2, 3), preferred_element_type=F32))
    keep(1, shared1)
    need("p1")

    def settle_base(tile):
        update(1, tile)
        upd[tile] = held[tile].astype(BF16)

    settle_base(after(2))
    relayed = [fold_far(upd, folds[2], i, 2) for i in range(2)]
    settle_base(after(1))
    settle_base(after(n_leaf - 1))
    direct = fold_near(upd, folds[2])
    update(1, x)
    _, spread3 = solve(3, merge3)
    last = []
    for i in range(2):
        relayed[i].wait()
        last.append(fold_on(upd, folds[2], i, 2))
    shared = share(2, spread2)
    sum_tiles(2, (direct2, last2))
    sum_tiles(3, (direct3, last3))
    keep(2, shared)
    for arrival in (direct, *last):
        arrival.wait()
    half = rhs // 2
    for i in range(2):
        acc[i] = folded(held[x], folds[2], i)
    for i in range(2):
        acc[i] = take(2, i)
    fin, got = folds[3]
    shared = share(3, spread3)
    quarter = half // 2
    early, late = pl.ds(0, quarter), pl.ds(quarter, quarter)

    def send(src, dst, dev):
        return exchange([(src, dst, dev)], src)

    def rows(i):
        return pl.ds(pl.multiple_of(i * half, half), half)

    fin[c] = take(3, c).astype(BF16)
    to_up = send(fin.at[c], got.at[0, c], up)
    others = [send(fin.at[c, early], got.at[1, c, early], down)]
    keep(3, shared)
    fin[1 - c] = take(3, 1 - c).astype(BF16)
    to_down = send(fin.at[1 - c], got.at[1, 1 - c], down)
    others.append(send(fin.at[c, late], got.at[1, c, late], down))
    others.append(send(fin.at[1 - c], got.at[0, 1 - c], up))
    for i in range(2):
        drains.append(fetch(fin.at[i], upd_o.at[x, rows(i)]))
    to_up.wait()
    passed = [send(got.at[0, c], upd_o.at[after(n_leaf - 1), rows(c)], up)]
    to_down.wait()
    passed.append(send(got.at[1, 1 - c], upd_o.at[after(1), rows(1 - c)], down))
    for arrival in others:
        arrival.wait()
    for k, origin in ((0, after(n_leaf - 1)), (1, after(1))):
        for i in range(2):
            drains.append(fetch(got.at[k, i], upd_o.at[origin, rows(i)]))
    for arrival in passed:
        arrival.wait()
    for copy in drains:
        copy.wait()


def settle(solved_h, updated_h, solved_o, updated_o, a, b, sem):
    ways = []
    for i, (src, mid, dst) in enumerate(((solved_h, a, solved_o), (updated_h, b, updated_o))):
        for k in range(src.shape[0]):
            spot = 2 * (i * src.shape[0] + k)
            ways.append(
                (
                    pltpu.make_async_copy(src.at[k], mid.at[k], sem.at[spot]),
                    pltpu.make_async_copy(mid.at[k], dst.at[k], sem.at[spot + 1]),
                )
            )
    for into, _ in ways:
        into.start()
    for into, out in ways:
        into.wait()
        out.start()
    for _, out in ways:
        out.wait()


def on_device(grid, n_leaf, right_side, panels, tile_counts, diag_leaf, diag_pair, diag_root, sup_rows):
    ny, nz, nc = grid
    levels, _, tiles, wide, _ = panels.shape
    rhs = right_side.shape[2]
    mid, part, low = rhs // nc, rhs // nc // nz, wide // ny
    step = wide // nc // nz
    slices, floods = [], []
    for m in range(levels):
        spread = [((nz, part), wide)] if m < 2 else [((ny, mid), low), ((nz, part), low)]
        slices.append([pltpu.VMEM((nc, mid, wide), BF16), pltpu.VMEM((mid, wide), BF16)])
        for (ways, rows), length in spread:
            slices[m] += [pltpu.VMEM((ways, rows, length), BF16), pltpu.VMEM((ways - 1, rows, length), BF16)]
        piece, kind = ((part, wide), BF16) if m < 2 else ((part, low), F32)
        floods.append([pltpu.VMEM(piece, kind), pltpu.VMEM((meeting(m, n_leaf) * ny, *piece), kind)])
    pub = [
        [
            pltpu.VMEM((nc, pairs, wide // nc, wide), BF16),
            pltpu.VMEM((pairs, wide // nc, wide), BF16),
            pltpu.VMEM((ny, pairs, wide // nc, low), BF16),
            pltpu.VMEM((ny - 1, pairs, wide // nc, low), BF16),
            pltpu.VMEM((nz, pairs, step, low), BF16),
            pltpu.VMEM((nz - 1, pairs, step, low), BF16),
            pltpu.VMEM((nc, nz, pairs, step, low), BF16),
        ]
        for pairs in map(len, BATCHES)
    ]
    scratch = [
        pltpu.VMEM((tiles, rhs, wide), BF16),
        [pltpu.VMEM((tiles, wide, wide), BF16)] * levels,
        pltpu.VMEM((1, wide, wide), BF16),
        pltpu.VMEM((2, wide, wide), BF16),
        pltpu.VMEM((2, wide, wide), BF16),
        pltpu.VMEM((tiles, rhs, wide), F32),
        [pltpu.VMEM((levels - 1, wide, wide), BF16)] * 2,
        pltpu.VMEM((levels, nc, nz, part, wide), BF16),
        [pltpu.VMEM((tiles, wide, wide), BF16)] * 2,
        pltpu.VMEM((2, wide, wide), BF16),
        pltpu.VMEM((2, mid, wide), F32),
        pltpu.VMEM((tiles, rhs, wide), BF16),
        [[pltpu.VMEM((2, length // 2, wide), BF16)] * 4 for length in (wide, wide, rhs)]
        + [[pltpu.VMEM((2, rhs // 2, wide), BF16), pltpu.VMEM((2, 2, rhs // 2, wide), BF16)]],
        slices,
        floods,
        pub,
        pltpu.SemaphoreType.DMA((SEMS,)),
    ]
    anywhere, scalars = pl.BlockSpec(memory_space=pl.ANY), pl.BlockSpec(memory_space=pltpu.SMEM)
    solved, updated = pl.pallas_call(
        functools.partial(kernel, grid, n_leaf),
        out_shape=(
            jax.ShapeDtypeStruct((levels, nc, nz, part, wide), BF16),
            jax.ShapeDtypeStruct((tiles, rhs, wide), BF16),
        ),
        in_specs=[scalars, scalars] + [anywhere] * 5,
        out_specs=(anywhere, anywhere),
        scratch_shapes=scratch,
        compiler_params=pltpu.CompilerParams(
            collective_id=0, has_side_effects=True, vmem_limit_bytes=56 * 2**20
        ),
    )(sup_rows, tile_counts, right_side, panels, diag_leaf, diag_pair, diag_root)
    shapes = [solved.shape, updated.shape]
    solved, updated = pl.pallas_call(
        settle,
        out_shape=tuple(jax.ShapeDtypeStruct(shape, BF16) for shape in shapes),
        in_specs=[anywhere] * 2,
        out_specs=(anywhere, anywhere),
        scratch_shapes=[pltpu.VMEM(shape, BF16) for shape in shapes]
        + [pltpu.SemaphoreType.DMA((2 * (levels + tiles),))],
        compiler_params=pltpu.CompilerParams(vmem_limit_bytes=56 * 2**20),
    )(solved, updated)
    return solved.reshape(levels, 1, rhs, wide), updated


def solution(mesh):
    placed = (
        P("leaf", "row", None, None),
        P(None, "leaf", "row", None, None),
        P(None, "leaf", "row"),
        P("leaf", None, None),
        P(),
        P(),
        P(),
    )
    return jax.shard_map(
        functools.partial(on_device, GRIDS[mesh.shape["row"]], mesh.shape["leaf"]),
        mesh=mesh,
        in_specs=placed,
        out_specs=(P(None, "leaf", None, None), P("row", None, None)),
        check_vma=False,
    )
```

```python
import functools

import jax
import jax.numpy as jnp
from jax import lax
from jax.experimental import pallas as pl
from jax.experimental.pallas import tpu as pltpu
from jax.sharding import PartitionSpec as P

MESH = pl.DeviceIdType.MESH
F32, BF16 = jnp.float32, jnp.bfloat16
BATCHES = (((1, 2),), ((1, 3), (2, 3)))
GRIDS = {64: (4, 8, 2), 8: (2, 2, 2)}
SEMS = 128


def meeting(level, n_leaf):
    return (1, 2, n_leaf, n_leaf)[level]


def kernel(grid, n_leaf, sup, cnt, rs_h, pan_h, dl_h, dp_h, dr_h, sol_o, upd_o, *scratch):
    ny, nz, nc = grid
    (rs, pan, dl, dp, dr, held, first, sol, live, sums, acc, upd, folds, slices, floods, pub, sem) = scratch
    levels, (tiles, wide, _) = len(pan), pan[0].shape
    rhs = rs.shape[1]
    low, mid, part = wide // ny, rhs // nc, rhs // nc // nz
    x, r = lax.axis_index("leaf"), lax.axis_index("row")
    y, z, c = r // (nz * nc), (r // nc) % nz, r % nc
    used = [0]
    drains = []

    def device(x_, y_, z_, c_):
        return (x_, (y_ * nz + z_) * nc + c_)

    def fresh():
        used[0] += 1
        assert used[0] <= SEMS
        return sem.at[used[0] - 1]

    def fetch(src, dst):
        copy = pltpu.make_async_copy(src, dst, fresh())
        copy.start()
        return copy

    def exchange(copies, whole):
        out, got = fresh(), fresh()
        for src, dst, dev in copies:
            pltpu.make_async_remote_copy(
                src_ref=src, dst_ref=dst, send_sem=out, recv_sem=got, device_id=dev, device_id_type=MESH
            ).start()
        drains.append(pltpu.make_async_copy(whole, whole, out))
        return pltpu.make_async_copy(whole, whole, got)

    def to_core(src, dst):
        return exchange([(src, dst, device(x, y, z, 1 - c))], dst)

    def scatter_z(src, dst):
        return exchange([(src.at[(z + k) % nz], dst.at[k - 1], device(x, y, (z + k) % nz, c)) for k in range(1, nz)], dst)

    def scatter_y(src, dst):
        return exchange([(src.at[(y + k) % ny], dst.at[k - 1], device(x, (y + k) % ny, z, c)) for k in range(1, ny)], dst)

    def gather_z(ref):
        return exchange(
            [(ref.at[z], ref.at[z], device(x, y, (z + k) % nz, c)) for k in range(1, nz)], ref.at[pl.ds(0, nz - 1)]
        )

    def total(mine, others):
        value = mine.astype(F32)
        for k in range(others.shape[0]):
            value = value + others[k].astype(F32)
        return value

    ready = {"rs": fetch(rs_h.at[0], rs)}
    barrier = pltpu.get_barrier_semaphore()
    peers = [device(x, y, (z + k) % nz, c) for k in sorted(range(1, nz), key=lambda k: abs(k - nz // 2))]
    peers += [device(x ^ i, (y + j) % ny, z, c) for i in range(n_leaf) for j in range(ny) if i or j]
    peers += [device(x, y, z, 1 - c)]
    for dev in peers:
        pl.semaphore_signal(barrier, inc=1, device_id=dev, device_id_type=MESH)

    ready["d0"] = fetch(dl_h, dl)
    for level, name in ((1, "p1"), (2, "p2"), (3, "p3"), (0, "p0")):
        ready[name] = fetch(pan_h.at[level, 0], pan[level])
    ready["d1"] = fetch(dp_h, dp)
    ready["d2"] = fetch(dr_h, dr)
    waited = set()

    def need(name):
        if name not in waited:
            waited.add(name)
            ready[name].wait()

    owner = [jnp.where(lax.div(sup[m], tiles) == r, 1.0, 0.0).astype(F32) for m in range(levels)]
    local = [lax.rem(sup[m], tiles) for m in range(levels)]
    columns = lax.broadcasted_iota(jnp.int32, (1, wide), 1)

    def product(level, tile, count):
        done = sol[level].reshape(rhs, wide)
        term = jnp.dot(done, pan[level][tile], preferred_element_type=F32)
        return jnp.where(columns < count, term, 0.0)

    def update(level, tile):
        count = cnt[level, 0, tile]
        for m in range(level + 1):
            count = jnp.where(sup[m] == r * tiles + tile, 0, count)
        term = product(level, tile, count)
        before = rs[tile].astype(F32) if level == 0 else held[tile]
        held[tile] = before - term

    def bulk(level):
        need(f"p{level}")

        def one(tile, carry):
            update(level, tile)
            return carry

        lax.fori_loop(0, tiles, one, 0)

    def prepare(m):
        qs = slices[m][0]
        rows = rs[local[m]] * owner[m].astype(BF16)
        for half in range(nc):
            qs[half] = rows[half * mid : (half + 1) * mid]

    def begin(m):
        qs, qr = slices[m][:2]
        return to_core(qs.at[1 - c], qr)

    def columns_y(m, arrival):
        ys, yr = slices[m][2:4]
        both = half_of(m, arrival)
        for k in range(ny):
            ys[k] = both[:, k * low : (k + 1) * low]
        return scatter_y(ys, yr)

    def rows_z(m, arrival):
        ys, yr, zs, zr = slices[m][2:]
        arrival.wait()
        zs[...] = total(ys[y], yr).astype(BF16).reshape(nz, part, low)
        return scatter_z(zs, zr)

    def piece_of(m, arrival):
        zs, zr = slices[m][4:]
        arrival.wait()
        return total(zs[z], zr)

    def half_of(m, arrival):
        qs, qr = slices[m][:2]
        arrival.wait()
        both = qs[c].astype(F32) + qr[...].astype(F32)
        if m:
            both = both - jnp.dot(sol[0, c].reshape(mid, wide), first[1][m - 1], preferred_element_type=F32)
        return both.astype(BF16)

    def slice_z(m, arrival):
        zs, zr = slices[m][2:4]
        zs[...] = half_of(m, arrival).reshape(nz, part, wide)
        return scatter_z(zs, zr)

    def rows_of(m, arrival):
        zs, zr = slices[m][2:4]
        arrival.wait()
        return total(zs[z], zr).astype(BF16)

    def flood(m, value):
        n = meeting(m, n_leaf)
        cs, cr = floods[m]
        own = (x % n) * ny + y
        value = value.astype(BF16)
        cs[...] = value
        cr[own] = value
        return exchange(
            [(cs, cr.at[own], device(x ^ a, (y + b) % ny, z, c)) for a in range(n) for b in range(ny) if a or b],
            cr.at[pl.ds(0, n * ny - 1)],
        )

    def solve(m, arrival):
        n = meeting(m, n_leaf)
        cr = floods[m][1]
        arrival.wait()
        if m < 2:
            merged = cr[0].astype(F32)
            for k in range(1, n * ny):
                merged = merged + cr[k].astype(F32)
            merged = merged.astype(BF16)
        else:
            parts = []
            for k in range(ny):
                value = cr[k].astype(F32)
                for a in range(1, n):
                    value = value + cr[a * ny + k].astype(F32)
                parts.append(value.astype(BF16))
            merged = jnp.concatenate(parts, axis=1)
        need(("d0", "d1", "d2", "d2")[m])
        inverse = dl[0] if m == 0 else dp[x // 2] if m == 1 else dr[m - 2]
        solved = jnp.dot(merged, inverse, preferred_element_type=F32).astype(BF16)
        sol[m, c, z] = solved
        return solved, gather_z(sol.at[m, c])

    def share(m, arrival):
        arrival.wait()
        return to_core(sol.at[m, c], sol.at[m, c])

    def keep(m, arrival):
        arrival.wait()
        drains.append(fetch(sol.at[m], sol_o.at[m]))

    def first_core():
        need("p0")
        for m in range(1, levels):
            alive = jnp.where(columns < cnt[0, 0, local[m]], owner[m], 0.0).astype(BF16)
            first[0][m - 1] = pan[0][local[m]] * alive
        return to_core(first[0], first[1])

    def publish_prepare(batch):
        pc = pub[batch][0]
        for i, (level, m) in enumerate(BATCHES[batch]):
            need(f"p{level}")
            alive = jnp.where(columns < cnt[level, 0, local[m]], owner[m], 0.0).astype(BF16)
            tile = pan[level][local[m]] * alive
            for half in range(nc):
                pc[half, i] = tile[half * (wide // nc) : (half + 1) * (wide // nc)]

    def publish_core(batch):
        pc, pcr = pub[batch][:2]
        return to_core(pc.at[1 - c], pcr)

    def publish_y(batch, arrival):
        pc, pcr, py, pyr = pub[batch][:4]
        arrival.wait()
        for i in range(len(BATCHES[batch])):
            both = (pc[c, i].astype(F32) + pcr[i].astype(F32)).astype(BF16)
            for k in range(ny):
                py[k, i] = both[:, k * low : (k + 1) * low]
        return scatter_y(py, pyr)

    def publish_z(batch, arrival):
        py, pyr, pz, pzr = pub[batch][2:6]
        arrival.wait()
        step = wide // nc // nz
        for i in range(len(BATCHES[batch])):
            value = py[y, i].astype(F32)
            for k in range(ny - 1):
                value = value + pyr[k, i].astype(F32)
            value = value.astype(BF16)
            for k in range(nz):
                pz[k, i] = value[k * step : (k + 1) * step]
        return scatter_z(pz, pzr)

    def publish_gather(batch, arrival):
        pz, pzr, pf = pub[batch][4:]
        arrival.wait()
        pf[c, z] = total(pz[z], pzr).astype(BF16)
        return gather_z(pf.at[c])

    def publish_last(batch, arrival):
        pf = pub[batch][6]
        arrival.wait()
        return to_core(pf.at[c], pf.at[c])

    def coupling(level, m):
        batch = 0 if (level, m) in BATCHES[0] else 1
        return pub[batch][6][:, :, BATCHES[batch].index((level, m))].reshape(wide, low)

    def after(k):
        return (x + k) % n_leaf

    up, down = device(after(1), y, z, c), device(after(n_leaf - 1), y, z, c)

    def fold_far(src, bufs, piece=0, pieces=1):
        relay = bufs[0]
        half, size = relay.shape[1], relay.shape[1] // pieces
        far, rows, second = after(2), pl.ds(piece * size, size), pl.ds(half + piece * size, size)
        return exchange(
            [(src.at[far, rows], relay.at[0, rows], up), (src.at[far, second], relay.at[1, rows], down)],
            relay.at[:, rows],
        )

    def fold_near(src, bufs):
        near = bufs[1]
        half = near.shape[1]
        first, second = pl.ds(0, half), pl.ds(half, half)
        return exchange(
            [(src.at[after(1), second], near.at[1], up), (src.at[after(n_leaf - 1), first], near.at[0], down)], near
        )

    def fold_on(src, bufs, piece=0, pieces=1):
        relay, _, out, last = bufs
        half, size = relay.shape[1], relay.shape[1] // pieces
        a, b = piece * size, (piece + 1) * size
        out[0, a:b] = (src[after(1), a:b].astype(F32) + relay[0, a:b].astype(F32)).astype(BF16)
        out[1, a:b] = (src[after(n_leaf - 1), half + a : half + b].astype(F32) + relay[1, a:b].astype(F32)).astype(BF16)
        rows = pl.ds(a, size)
        return exchange([(out.at[0, rows], last.at[0, rows], up), (out.at[1, rows], last.at[1, rows], down)], last.at[:, rows])

    def folded(mine, bufs, i):
        _, near, _, last = bufs
        half = near.shape[1]
        return mine[i * half : (i + 1) * half].astype(F32) + near[i].astype(F32) + last[i].astype(F32)

    def mask_tiles(level):
        need(f"p{level}")
        into = live[level - 2]

        def one(tile, carry):
            count = cnt[level, 0, tile]
            for m in range(level + 1):
                count = jnp.where(sup[m] == r * tiles + tile, 0, count)
            into[tile] = pan[level][tile] * jnp.where(columns < count, 1.0, 0.0).astype(BF16)
            return carry

        lax.fori_loop(0, tiles, one, 0)

    def sum_tiles(level, arrivals):
        for arrival in arrivals:
            arrival.wait()
        half = wide // 2
        for i in range(2):
            sums[level - 2, i * half : (i + 1) * half] = folded(live[level - 2][x], folds[level - 2], i).astype(BF16)

    def take(level, half):
        done = sol[level, half].reshape(mid, wide)
        return acc[half] - jnp.dot(done, sums[level - 2], preferred_element_type=F32)

    need("rs")
    prepare(0)
    pl.semaphore_wait(barrier, len(peers))
    arrival = begin(0)
    publish_prepare(0)
    pub_a = publish_core(0)
    mask_tiles(3)
    relayed3 = fold_far(live[1], folds[1])
    direct3 = fold_near(live[1], folds[1])
    arrival = slice_z(0, arrival)
    publish_prepare(1)
    pub_b = publish_core(1)
    arrivals = {}
    for m in (1, 2, 3):
        prepare(m)
        arrivals[m] = begin(m)
    pub_a = publish_y(0, pub_a)
    coupled = first_core()
    arrival = flood(0, rows_of(0, arrival))
    pub_b = publish_y(1, pub_b)
    pub_a = publish_z(0, pub_a)
    mask_tiles(2)
    relayed3.wait()
    last3 = fold_on(live[1], folds[1])
    relayed2 = fold_far(live[0], folds[0])
    _, arrival = solve(0, arrival)
    coupled.wait()
    for m in range(1, levels):
        first[1][m - 1] = first[0][m - 1] + first[1][m - 1]
    pub_a = publish_gather(0, pub_a)
    shared0 = share(0, arrival)
    arrivals[1] = slice_z(1, arrivals[1])
    arrivals[2] = columns_y(2, arrivals[2])
    pub_b = publish_z(1, pub_b)
    arrivals[3] = columns_y(3, arrivals[3])
    pub_a = publish_last(0, pub_a)
    keep(0, shared0)
    bulk(0)
    merge1 = flood(1, rows_of(1, arrivals[1]))
    for m in (2, 3):
        arrivals[m] = rows_z(m, arrivals[m])
    direct2 = fold_near(live[0], folds[0])
    pub_b = publish_gather(1, pub_b)
    solved1, spread1 = solve(1, merge1)
    pub_a.wait()
    piece = piece_of(2, arrivals[2])
    merge2 = flood(2, piece - jnp.dot(solved1, coupling(1, 2), preferred_element_type=F32))
    relayed2.wait()
    last2 = fold_on(live[0], folds[0])
    pub_b = publish_last(1, pub_b)
    piece = piece_of(3, arrivals[3])
    pub_b.wait()
    piece = piece - jnp.dot(solved1, coupling(1, 3), preferred_element_type=F32)
    shared1 = share(1, spread1)
    solved2, spread2 = solve(2, merge2)
    merge3 = flood(3, piece - jnp.dot(solved2, coupling(2, 3), preferred_element_type=F32))
    keep(1, shared1)
    need("p1")

    def settle_base(tile):
        update(1, tile)
        upd[tile] = held[tile].astype(BF16)

    settle_base(after(2))
    relayed = [fold_far(upd, folds[2], i, 2) for i in range(2)]
    settle_base(after(1))
    settle_base(after(n_leaf - 1))
    direct = fold_near(upd, folds[2])
    update(1, x)
    _, spread3 = solve(3, merge3)
    last = []
    for i in range(2):
        relayed[i].wait()
        last.append(fold_on(upd, folds[2], i, 2))
    shared = share(2, spread2)
    sum_tiles(2, (direct2, last2))
    sum_tiles(3, (direct3, last3))
    keep(2, shared)
    for arrival in (direct, *last):
        arrival.wait()
    half = rhs // 2
    for i in range(2):
        acc[i] = folded(held[x], folds[2], i)
    for i in range(2):
        acc[i] = take(2, i)
    fin, got = folds[3]
    shared = share(3, spread3)
    quarter = half // 2
    early, late = pl.ds(0, quarter), pl.ds(quarter, quarter)

    def send(src, dst, dev):
        return exchange([(src, dst, dev)], src)

    def rows(i):
        return pl.ds(pl.multiple_of(i * half, half), half)

    fin[c] = take(3, c).astype(BF16)
    to_up = send(fin.at[c], got.at[0, c], up)
    others = [send(fin.at[c, early], got.at[1, c, early], down)]
    keep(3, shared)
    fin[1 - c] = take(3, 1 - c).astype(BF16)
    to_down = send(fin.at[1 - c], got.at[1, 1 - c], down)
    others.append(send(fin.at[c, late], got.at[1, c, late], down))
    others.append(send(fin.at[1 - c], got.at[0, 1 - c], up))
    for i in range(2):
        drains.append(fetch(fin.at[i], upd_o.at[x, rows(i)]))
    to_up.wait()
    passed = [send(got.at[0, c], upd_o.at[after(n_leaf - 1), rows(c)], up)]
    to_down.wait()
    passed.append(send(got.at[1, 1 - c], upd_o.at[after(1), rows(1 - c)], down))
    for arrival in others:
        arrival.wait()
    for k, origin in ((0, after(n_leaf - 1)), (1, after(1))):
        for i in range(2):
            drains.append(fetch(got.at[k, i], upd_o.at[origin, rows(i)]))
    for arrival in passed:
        arrival.wait()
    for copy in drains:
        copy.wait()


def settle(solved_h, updated_h, solved_o, updated_o, a, b, sem):
    ways = []
    for i, (src, mid, dst) in enumerate(((solved_h, a, solved_o), (updated_h, b, updated_o))):
        for k in range(src.shape[0]):
            spot = 2 * (i * src.shape[0] + k)
            ways.append(
                (
                    pltpu.make_async_copy(src.at[k], mid.at[k], sem.at[spot]),
                    pltpu.make_async_copy(mid.at[k], dst.at[k], sem.at[spot + 1]),
                )
            )
    for into, _ in ways:
        into.start()
    for into, out in ways:
        into.wait()
        out.start()
    for _, out in ways:
        out.wait()


def on_device(grid, n_leaf, right_side, panels, tile_counts, diag_leaf, diag_pair, diag_root, sup_rows):
    ny, nz, nc = grid
    levels, _, tiles, wide, _ = panels.shape
    rhs = right_side.shape[2]
    mid, part, low = rhs // nc, rhs // nc // nz, wide // ny
    step = wide // nc // nz
    slices, floods = [], []
    for m in range(levels):
        spread = [((nz, part), wide)] if m < 2 else [((ny, mid), low), ((nz, part), low)]
        slices.append([pltpu.VMEM((nc, mid, wide), BF16), pltpu.VMEM((mid, wide), BF16)])
        for (ways, rows), length in spread:
            slices[m] += [pltpu.VMEM((ways, rows, length), BF16), pltpu.VMEM((ways - 1, rows, length), BF16)]
        piece = (part, wide) if m < 2 else (part, low)
        floods.append([pltpu.VMEM(piece, BF16), pltpu.VMEM((meeting(m, n_leaf) * ny, *piece), BF16)])
    pub = [
        [
            pltpu.VMEM((nc, pairs, wide // nc, wide), BF16),
            pltpu.VMEM((pairs, wide // nc, wide), BF16),
            pltpu.VMEM((ny, pairs, wide // nc, low), BF16),
            pltpu.VMEM((ny - 1, pairs, wide // nc, low), BF16),
            pltpu.VMEM((nz, pairs, step, low), BF16),
            pltpu.VMEM((nz - 1, pairs, step, low), BF16),
            pltpu.VMEM((nc, nz, pairs, step, low), BF16),
        ]
        for pairs in map(len, BATCHES)
    ]
    scratch = [
        pltpu.VMEM((tiles, rhs, wide), BF16),
        [pltpu.VMEM((tiles, wide, wide), BF16)] * levels,
        pltpu.VMEM((1, wide, wide), BF16),
        pltpu.VMEM((2, wide, wide), BF16),
        pltpu.VMEM((2, wide, wide), BF16),
        pltpu.VMEM((tiles, rhs, wide), F32),
        [pltpu.VMEM((levels - 1, wide, wide), BF16)] * 2,
        pltpu.VMEM((levels, nc, nz, part, wide), BF16),
        [pltpu.VMEM((tiles, wide, wide), BF16)] * 2,
        pltpu.VMEM((2, wide, wide), BF16),
        pltpu.VMEM((2, mid, wide), F32),
        pltpu.VMEM((tiles, rhs, wide), BF16),
        [[pltpu.VMEM((2, length // 2, wide), BF16)] * 4 for length in (wide, wide, rhs)]
        + [[pltpu.VMEM((2, rhs // 2, wide), BF16), pltpu.VMEM((2, 2, rhs // 2, wide), BF16)]],
        slices,
        floods,
        pub,
        pltpu.SemaphoreType.DMA((SEMS,)),
    ]
    anywhere, scalars = pl.BlockSpec(memory_space=pl.ANY), pl.BlockSpec(memory_space=pltpu.SMEM)
    solved, updated = pl.pallas_call(
        functools.partial(kernel, grid, n_leaf),
        out_shape=(
            jax.ShapeDtypeStruct((levels, nc, nz, part, wide), BF16),
            jax.ShapeDtypeStruct((tiles, rhs, wide), BF16),
        ),
        in_specs=[scalars, scalars] + [anywhere] * 5,
        out_specs=(anywhere, anywhere),
        scratch_shapes=scratch,
        compiler_params=pltpu.CompilerParams(
            collective_id=0, has_side_effects=True, vmem_limit_bytes=56 * 2**20
        ),
    )(sup_rows, tile_counts, right_side, panels, diag_leaf, diag_pair, diag_root)
    shapes = [solved.shape, updated.shape]
    solved, updated = pl.pallas_call(
        settle,
        out_shape=tuple(jax.ShapeDtypeStruct(shape, BF16) for shape in shapes),
        in_specs=[anywhere] * 2,
        out_specs=(anywhere, anywhere),
        scratch_shapes=[pltpu.VMEM(shape, BF16) for shape in shapes]
        + [pltpu.SemaphoreType.DMA((2 * (levels + tiles),))],
        compiler_params=pltpu.CompilerParams(vmem_limit_bytes=56 * 2**20),
    )(solved, updated)
    return solved.reshape(levels, 1, rhs, wide), updated


def solution(mesh):
    placed = (
        P("leaf", "row", None, None),
        P(None, "leaf", "row", None, None),
        P(None, "leaf", "row"),
        P("leaf", None, None),
        P(),
        P(),
        P(),
    )
    return jax.shard_map(
        functools.partial(on_device, GRIDS[mesh.shape["row"]], mesh.shape["leaf"]),
        mesh=mesh,
        in_specs=placed,
        out_specs=(P(None, "leaf", None, None), P("row", None, None)),
        check_vma=False,
    )
```
